128 devices in a mesh: island: 4 (over x), expert: 16 (over z, y), tensor: 2 (over core).
Axes of the slice: x: 4, y: 4, z: 4, core: 2. Of those that a mesh axis runs over, the one named last changes fastest.
Arguments:
- tokens: bfloat16 [4, 4096, 2048], P('island', 'expert', 'tensor'), may hold values from -6 to 6
- token_grads: bfloat16 [4, 4096, 2048], P('island', 'expert', 'tensor'), may hold values from -6 to 6
- slot_token: int32 [4, 16, 16, 96], P('island', 'expert'), may hold values from 0 to 255, as said below
- slot_count: int32 [4, 16, 16], P('island', 'expert'), may hold values from 24 to 96, as said below
- slot_prob: float32 [4, 16, 16, 96], P('island', 'expert'), may hold values from 0.1 to 1
- gate_weight: bfloat16 [4, 16, 2048, 1536], P('island', 'expert', None, 'tensor'), may hold values from -0.125 to 0.125
- down_weight: bfloat16 [4, 16, 1536, 2048], P('island', 'expert', 'tensor'), may hold values from -0.15625 to 0.15625
- drift: bfloat16 [4, 16, 2048, 1536], P('island', 'expert', None, 'tensor'), may hold values from -6 to 6
- momentum: float32 [16, 2048, 1536], P('expert', None, 'tensor'), may hold values from -1.5 to 1.5
Outputs:
- new_momentum: float32 [16, 2048, 1536], P('expert', None, 'tensor')
- outer_step: bfloat16 [16, 2048, 1536], P('expert', None, 'tensor')
The draws below stay inside these ranges and needn't reach their ends.
Inputs may be any that keep to these rules, and one draw needn't show every extreme that they name: `slot_token`: for each island, source device and expert the 96 entries are distinct tokens of that source device. `slot_count`: in every island some expert is full from every source device.
All inputs are finite; a program needn't handle non-finite values.
Results may differ from the reference program's by a relative error of at most 0.0031.
The reference program's roundings to bfloat16 on the way (of `input_slots`, `grad_slots` and `hidden_grad`) count: a program that leaves them out, or rounds other values in their place, can miss the bound.
Values may be sent and summed in bfloat16 or wider, within the bound.
A program may use at most 128 MiB of HBM per device.

```python
import math
import jax
import jax.numpy as jnp
from jax import lax

D = 2048
FF = 1536
TOK_DEV = 256
CAP = 96
ISLANDS = 4
SOURCES = 16
EXPERTS = 16
TOKENS = 4096
ROWS = 1536


def draw_slot_token(key, part):
    row_count = ISLANDS * SOURCES * EXPERTS
    scores = jax.random.randint(key, (row_count, TOK_DEV), 0, 1 << 20) * TOK_DEV + jnp.arange(TOK_DEV, dtype=jnp.int32)[None, :]
    ranking = jnp.argsort(scores, axis=1, stable=True)[:, :CAP]
    return ranking.astype(jnp.int32).reshape(ISLANDS, SOURCES, EXPERTS, CAP)


def draw_slot_count(key, part):
    counts_drawn = jax.random.randint(jax.random.fold_in(key, 1), (ISLANDS, SOURCES, EXPERTS), CAP // 4, CAP + 1)
    full_expert = jax.random.randint(jax.random.fold_in(key, 2), (ISLANDS, 1, 1), 0, EXPERTS)
    chosen = jnp.arange(EXPERTS, dtype=jnp.int32)[None, None, :] == full_expert
    return jnp.where(chosen, CAP, counts_drawn).astype(jnp.int32)


def strengthened(result, rng, source, target, parts, factor):
    def block_of(dim):
        return (jnp.arange(result.shape[dim]) // (result.shape[dim] // parts)).reshape((-1,) + (1,) * (result.ndim - 1 - dim))

    near = jax.random.permutation(rng, parts)[block_of(target)]
    other_side = (block_of(target) + parts // 2) % parts
    return jnp.where((block_of(source) == near) | (block_of(source) == other_side), factor * result, result)


def block_scale(key, shape, cuts, least, high):
    factor_of = 1.0
    for axis_at, shards_of in cuts:
        heights = jax.random.uniform(jax.random.fold_in(jax.random.fold_in(key, 6), axis_at), (shards_of,), jnp.float32, least / len(cuts), high / len(cuts))
        factor_of = factor_of * jnp.repeat(jnp.exp(heights), shape[axis_at] // shards_of).reshape((-1,) + (1,) * (len(shape) - 1 - axis_at))
    return factor_of


def normal_values(stream_key, dims, width, limit, cuts=(), kind=jnp.bfloat16):
    loudness = block_scale(stream_key, dims, cuts, -0.22, 0.18) if cuts else 1.0
    drawn = jax.random.normal(stream_key, dims, jnp.float32) * width * loudness
    return jnp.minimum(jnp.maximum(drawn, -limit), limit).astype(kind)


def bell_draw_with(stream_key, dims, width, most, cuts, heavy, kind=jnp.bfloat16):
    entries = width * jax.random.normal(stream_key, dims, jnp.float32)
    if cuts:
        entries = entries * block_scale(stream_key, dims, cuts, -0.22, 0.18)
    return jnp.clip(strengthened(entries, jax.random.fold_in(stream_key, 3), *heavy), -most, most).astype(kind)


def setup_inputs(seed: int = 0) -> dict:
    key_list = jax.random.split(jax.random.key(seed), 10)
    return {
        "tokens": normal_values(key_list[0], (ISLANDS, TOKENS, D), 1.0, 6.0, ((0, 4), (1, 16), (2, 2))),
        "token_grads": normal_values(key_list[1], (ISLANDS, TOKENS, D), 1.0, 6.0, ((0, 4), (1, 16), (2, 2))),
        "slot_token": draw_slot_token(jax.random.fold_in(key_list[9], 71), 0),
        "slot_count": draw_slot_count(jax.random.fold_in(key_list[9], 71), 0),
        "slot_prob": jnp.clip(0.1 + 0.9 * jax.random.uniform(key_list[4], (ISLANDS, SOURCES, EXPERTS, CAP), jnp.float32) ** block_scale(key_list[4], (ISLANDS, SOURCES, EXPERTS, CAP), ((0, 4), (1, 16)), -0.2, 0.2), 0.1, 1.0),
        "gate_weight": normal_values(key_list[5], (ISLANDS, EXPERTS, D, FF), D ** -0.5, 0.125, ((0, 4), (1, 16), (3, 2))),
        "down_weight": normal_values(key_list[6], (ISLANDS, EXPERTS, FF, D), FF ** -0.5, 0.15625, ((0, 4), (1, 16), (2, 2))),
        "drift": bell_draw_with(key_list[7], (ISLANDS, EXPERTS, D, FF), 1.0, 6.0, ((0, 4), (1, 16), (3, 2)), (0, 2, 4, 2.0)),
        "momentum": normal_values(key_list[8], (EXPERTS, D, FF), 0.25, 1.5, ((0, 16), (2, 2)), jnp.float32),
    }


def island_pseudo(island_tokens, island_grads, island_slots, island_counts, island_probs, island_gate, island_down, island_drift):
    offsets = (jnp.arange(SOURCES, dtype=jnp.int32) * TOK_DEV)[:, None, None]
    slot_rows = (island_slots + offsets).astype(jnp.int32)
    live_slots = jnp.arange(CAP, dtype=jnp.int32)[None, None, :] < island_counts[:, :, None]
    input_slots = jnp.where(live_slots[..., None], island_tokens[slot_rows], jnp.zeros((), jnp.bfloat16))
    slot_weights = jnp.where(live_slots, island_probs, jnp.float32(0.0))[..., None]
    grad_slots = (slot_weights * island_grads[slot_rows].astype(jnp.float32)).astype(jnp.bfloat16)
    input_slots = input_slots.transpose(1, 0, 2, 3).reshape(EXPERTS, ROWS, D)
    grad_slots = grad_slots.transpose(1, 0, 2, 3).reshape(EXPERTS, ROWS, D)
    inputs_wide = input_slots.astype(jnp.float32)
    gate_value = jnp.einsum('erd,edf->erf', inputs_wide, island_gate.astype(jnp.float32))
    back_grad = jnp.einsum('erd,efd->erf', grad_slots.astype(jnp.float32), island_down.astype(jnp.float32))
    hidden_grad = (back_grad * jax.nn.silu(gate_value)).astype(jnp.bfloat16)
    gradient = jnp.einsum('erd,erf->edf', inputs_wide, hidden_grad.astype(jnp.float32))
    square_sum = jnp.sum(gradient * gradient)
    inner_scale = jnp.minimum(1.0, math.sqrt(EXPERTS * D * FF) / jnp.sqrt(square_sum + 1e-06))
    return island_drift.astype(jnp.float32) + inner_scale * gradient

def reference(tokens, token_grads, slot_token, slot_count, slot_prob, gate_weight, down_weight, drift, momentum):

    def accumulate(running, pieces):
        return (running + island_pseudo(*pieces), None)
    start = jnp.zeros((EXPERTS, D, FF), jnp.float32)
    total, _ = lax.scan(accumulate, start, (tokens, token_grads, slot_token, slot_count, slot_prob, gate_weight, down_weight, drift))
    average = total / ISLANDS
    square_sum = jnp.sum(average * average)
    outer_scale = jnp.minimum(1.0, 0.25 * math.sqrt(EXPERTS * D * FF) / jnp.sqrt(square_sum + 1e-06))
    clipped = outer_scale * average
    new_momentum = 0.9 * momentum + clipped
    outer_step = (0.7 * (clipped + 0.9 * new_momentum)).astype(jnp.bfloat16)
    return (new_momentum, outer_step)
```

```python
import functools
import math

import jax
import jax.numpy as jnp
from jax import lax
from jax.experimental import pallas as pl
from jax.experimental.pallas import tpu as pltpu
from jax.sharding import PartitionSpec as P

MESH = pl.DeviceIdType.MESH
BF16 = jnp.bfloat16
F32 = jnp.float32
AVG = jnp.bfloat16
N = 4
CAP = 96
GROUP = N * CAP
ROWS = N * GROUP
TOK = 256
HALF = 1024
FEAT = 2 * HALF
QUART = FEAT // N
HID = 768
TILE = 256
ENTRIES = 16 * 2048 * 1536


def back(k):
    return (N - k) % N


def kernel(
    tok_ref, tg_ref, tab_ref, wg_ref, wd_ref, drift_ref,
    avg_ref, sq_ref,
    tok_z, tg_y, tab_z, tab_y, send_x, send_g, relay_x, relay_g, xs, gs, wg, wd,
    gate, backg, xt, hid, g_own, g_send, g_relay, g_recv, d_recv, avg_all,
    part, tiles, send_sem, recv_sem, local_sem,
):
    x = lax.axis_index("island")
    ex = lax.axis_index("expert")
    t = lax.axis_index("tensor")
    z, y = ex // N, lax.rem(ex, N)

    def at_x(k):
        return {"island": lax.rem(x + k, N)}

    def at_z(k):
        return {"expert": lax.rem(z + k, N) * N + y}

    def at_y(k):
        return {"expert": z * N + lax.rem(y + k, N)}

    partner = {"tensor": 1 - t}
    started = []
    local_count = [0]

    def push(src, dst, device):
        i = len(started)
        copy = pltpu.make_async_remote_copy(
            src_ref=src, dst_ref=dst, send_sem=send_sem.at[i], recv_sem=recv_sem.at[i],
            device_id=device, device_id_type=MESH,
        )
        copy.start()
        started.append(copy)
        return copy

    def fetch(src, dst):
        copy = pltpu.make_async_copy(src, dst, local_sem.at[local_count[0]])
        local_count[0] += 1
        copy.start()
        return copy

    own_tok = fetch(tok_ref, tok_z.at[0])
    own_tab = fetch(tab_ref, tab_z.at[0])
    own_tab2 = fetch(tab_ref, tab_y.at[0])
    own_tg = fetch(tg_ref, tg_y.at[0])
    own_half = pl.ds(pl.multiple_of(t * HALF, HALF), HALF)
    other_half = pl.ds(pl.multiple_of((1 - t) * HALF, HALF), HALF)
    loads = [
        fetch(wg_ref.at[own_half, :], wg.at[0]),
        fetch(wg_ref.at[other_half, :], wg.at[1]),
        fetch(wd_ref.at[:, own_half], wd.at[0]),
        fetch(wd_ref.at[:, other_half], wd.at[1]),
    ]

    def quarter(k):
        return pl.ds(pl.multiple_of(lax.rem(x + k, N) * QUART, QUART), QUART)

    own_drift = fetch(drift_ref.at[quarter(0), :], d_recv.at[0])

    barrier = pltpu.get_barrier_semaphore()
    peers = [at(k) for at in (at_x, at_y, at_z) for k in (1, 2, 3)] + [partner]
    for peer in peers:
        pl.semaphore_signal(barrier, inc=1, device_id=peer, device_id_type=MESH)
    pl.semaphore_wait(barrier, len(peers))

    tz = {k: push(tab_ref, tab_z.at[back(k)], at_z(k)) for k in (1, 3, 2)}
    ty = {k: push(tab_ref, tab_y.at[back(k)], at_y(k)) for k in (1, 3, 2)}
    tok_up = push(tok_ref, tok_z.at[3], at_z(1))
    tok_down = push(tok_ref, tok_z.at[1], at_z(3))
    tg_up = push(tg_ref, tg_y.at[3], at_y(1))
    tg_down = push(tg_ref, tg_y.at[1], at_y(3))
    drifts = [push(drift_ref.at[quarter(k), :], d_recv.at[back(k)], at_x(k)) for k in (2, 1, 3)]

    lane = lax.broadcasted_iota(jnp.int32, (CAP, 128), 1)
    token_of = lax.broadcasted_iota(jnp.int32, (CAP, TOK), 1).astype(F32)

    def column(tab, at):
        return jnp.sum(jnp.where(lane == at, tab, 0.0), axis=1, keepdims=True)

    def picked(tab, rows, expert, weighted):
        chosen = jnp.where(column(tab, expert) == token_of, 1.0, 0.0).astype(BF16)
        out = jnp.dot(chosen, rows, preferred_element_type=F32)
        if weighted:
            out = out * column(tab, expert + 16)
        return out.astype(BF16)

    chunk = {}
    relays = {}

    def scatter_x(kz):
        tab, rows = tab_z[kz], tok_z[kz]
        for ky in (2, 1, 3, 0):
            expert = z * N + lax.rem(y + ky, N)
            got = picked(tab, rows, expert, False)
            if ky == 0:
                xs[0, kz, 0] = got
                continue
            send_x[ky - 1, kz] = got
            src = send_x.at[ky - 1, kz]
            if ky == 2:
                way = 1 if kz in (0, 2) else 3
                relays["x", kz] = (push(src, relay_x.at[kz], at_y(way)), way)
            else:
                chunk["x", kz, back(ky)] = push(src, xs.at[0, kz, back(ky)], at_y(ky))

    def scatter_g(ky):
        tab, rows = tab_y[ky], tg_y[ky]
        for kz in (2, 1, 3, 0):
            expert = lax.rem(z + kz, N) * N + y
            got = picked(tab, rows, expert, True)
            if kz == 0:
                gs[0, ky, 0] = got
                continue
            send_g[kz - 1, ky] = got
            src = send_g.at[kz - 1, ky]
            if kz == 2:
                way = 1 if ky in (0, 2) else 3
                relays["g", ky] = (push(src, relay_g.at[ky], at_z(way)), way)
            else:
                chunk["g", ky, back(kz)] = push(src, gs.at[0, ky, back(kz)], at_z(kz))

    shared = {}

    def share(name, group, member):
        if member:
            chunk[name, group, member].wait_recv()
        buf = xs if name == "x" else gs
        shared[name, group, member] = push(
            buf.at[0, group, member], buf.at[1, group, member], partner
        )

    def relay(name, group):
        copy, way = relays[name, group]
        copy.wait_recv()
        if name == "x":
            chunk[name, group, 2] = push(relay_x.at[group], xs.at[0, group, 2], at_y(way))
        else:
            chunk[name, group, 2] = push(relay_g.at[group], gs.at[0, group, 2], at_z(way))

    def gate_group(kz):
        for m in range(N):
            shared["x", kz, m].wait_recv()

        @pl.loop(0, HID // TILE)
        def _(n):
            cols = pl.ds(pl.multiple_of(n * TILE, TILE), TILE)
            v = jnp.dot(xs[0, kz].reshape(GROUP, HALF), wg[0, :, cols], preferred_element_type=F32)
            v += jnp.dot(xs[1, kz].reshape(GROUP, HALF), wg[1, :, cols], preferred_element_type=F32)
            gate[kz, :, cols] = v / (1.0 + jnp.exp(-v))

        for h in range(2):

            @pl.loop(0, HALF // TILE)
            def _(n):
                at = pl.multiple_of(n * TILE, TILE)
                block = xs[h, kz, :, :, pl.ds(at, TILE)].reshape(GROUP, TILE)
                xt[pl.ds(pl.multiple_of(h * HALF + at, TILE), TILE), kz * GROUP : (kz + 1) * GROUP] = block.T

    nt = (((1,), (1,)), ((), ()))

    def back_group(ky):
        for m in range(N):
            shared["g", ky, m].wait_recv()

        @pl.loop(0, HID // TILE)
        def _(n):
            cols = pl.ds(pl.multiple_of(n * TILE, TILE), TILE)
            v = lax.dot_general(gs[0, ky].reshape(GROUP, HALF), wd[0, cols, :], nt, preferred_element_type=F32)
            v += lax.dot_general(gs[1, ky].reshape(GROUP, HALF), wd[1, cols, :], nt, preferred_element_type=F32)
            backg[ky, :, cols] = v

    def hidden(kz, ky):
        rows = slice(kz * GROUP + ky * CAP, kz * GROUP + (ky + 1) * CAP)
        hid[rows, :] = (backg[ky, kz * CAP : (kz + 1) * CAP, :] * gate[kz, ky * CAP : (ky + 1) * CAP, :]).astype(BF16)

    own_tok.wait()
    own_tab.wait()
    scatter_x(0)
    own_tg.wait()
    own_tab2.wait()
    scatter_g(0)
    share("x", 0, 0)
    share("g", 0, 0)

    tok_up.wait_recv()
    tok_relay_up = push(tok_z.at[3, pl.ds(0, TOK // 2)], tok_z.at[2, pl.ds(0, TOK // 2)], at_z(1))
    tg_up.wait_recv()
    tg_relay_up = push(tg_y.at[3, pl.ds(0, TOK // 2)], tg_y.at[2, pl.ds(0, TOK // 2)], at_y(1))
    tok_down.wait_recv()
    tok_relay_down = push(
        tok_z.at[1, pl.ds(TOK // 2, TOK // 2)], tok_z.at[2, pl.ds(TOK // 2, TOK // 2)], at_z(3)
    )
    tg_down.wait_recv()
    tg_relay_down = push(
        tg_y.at[1, pl.ds(TOK // 2, TOK // 2)], tg_y.at[2, pl.ds(TOK // 2, TOK // 2)], at_y(3)
    )
    for k in (3, 1):
        tz[back(k)].wait_recv()
        scatter_x(k)
        ty[back(k)].wait_recv()
        scatter_g(k)
        share("x", k, 0)
        share("g", k, 0)
    relay("x", 0)
    relay("g", 0)
    for m in (1, 3):
        share("x", 0, m)
        share("g", 0, m)
    tok_relay_up.wait_recv()
    tok_relay_down.wait_recv()
    tz[2].wait_recv()
    scatter_x(2)
    tg_relay_up.wait_recv()
    tg_relay_down.wait_recv()
    ty[2].wait_recv()
    scatter_g(2)
    share("x", 2, 0)
    share("g", 2, 0)
    for k in (3, 1):
        relay("x", k)
        relay("g", k)
    share("x", 0, 2)
    share("g", 0, 2)
    for load in loads:
        load.wait()
    gate_group(0)
    back_group(0)
    hidden(0, 0)
    for k in (3, 1):
        for m in (1, 3):
            share("x", k, m)
            share("g", k, m)
    relay("x", 2)
    relay("g", 2)
    for k in (3, 1):
        share("x", k, 2)
        share("g", k, 2)
    for k in (3, 1):
        gate_group(k)
        back_group(k)
    for kz in (0, 1, 3):
        for ky in (0, 1, 3):
            if kz or ky:
                hidden(kz, ky)
    for m in (1, 3, 2):
        share("x", 2, m)
        share("g", 2, m)
    gate_group(2)
    back_group(2)
    for k in (0, 1, 3):
        hidden(2, k)
        hidden(k, 2)
    hidden(2, 2)

    part[...] = jnp.zeros_like(part)

    def folded(v):
        s = jnp.sum(v.reshape(v.shape[0] // 8, 8, v.shape[1]), axis=0)
        return sum(s[:, i * 128 : (i + 1) * 128] for i in range(v.shape[1] // 128))

    def gradient(k, store):
        d = lax.rem(x + k, N)
        at = lax.rem(d // 2 + t, 2) * HALF + lax.rem(d, 2) * QUART
        rows = pl.ds(pl.multiple_of(at, QUART), QUART)

        @pl.loop(0, HID // TILE)
        def _(n):
            cols = pl.ds(pl.multiple_of(n * TILE, TILE), TILE)
            v = jnp.dot(xt[rows, :], hid[:, cols], preferred_element_type=F32)
            part[0] += folded(v * v)
            store(cols, v)

    def sending(j):
        def store(cols, v):
            g_send[j, :, cols] = v.astype(BF16)

        return store

    def keeping(cols, v):
        g_own[:, cols] = v

    top, low = pl.ds(0, QUART // 2), pl.ds(QUART // 2, QUART // 2)
    gradient(2, sending(0))
    far_up = push(g_send.at[0, top], g_relay.at[0], at_x(1))
    far_down = push(g_send.at[0, low], g_relay.at[1], at_x(3))
    gradient(1, sending(1))
    near_up = push(g_send.at[1], g_recv.at[3], at_x(1))
    gradient(3, sending(2))
    near_down = push(g_send.at[2], g_recv.at[1], at_x(3))
    gradient(0, keeping)

    slot = [0]

    def gathered(value, pushes):
        first = slot[0]
        slot[0] += 1 + len(pushes)
        tiles[first] = value
        copies = []
        for i, (device, place) in enumerate(pushes):
            copies.append(push(tiles.at[first], tiles.at[first + place], device))
        for copy in copies:
            copy.wait_recv()
        return [tiles[first + i] for i in range(1 + len(pushes))]

    def ring(at):
        return [(at(k), back(k)) for k in (1, 2, 3)]

    def summed(v):
        return (v[0] + v[2]) + (v[1] + v[3])

    def group_sum(value):
        a = gathered(value, [(partner, 1)])
        b = summed(gathered(a[0] + a[1], ring(at_z)))
        return summed(gathered(b, ring(at_y)))

    square = group_sum(part[0])
    far_up.wait_recv()
    far_up2 = push(g_relay.at[0], g_recv.at[2, top], at_x(1))
    far_down.wait_recv()
    far_down2 = push(g_relay.at[1], g_recv.at[2, low], at_x(3))
    squares = gathered(square, ring(at_x))
    scales = []
    for v in squares:
        total = jnp.sum(jnp.sum(v, axis=1, keepdims=True), axis=0, keepdims=True)
        scales.append(jnp.minimum(1.0, math.sqrt(ENTRIES) / jnp.sqrt(total + 1e-06)))

    own_drift.wait()
    for copy in drifts:
        copy.wait_recv()
    near_up.wait_recv()
    near_down.wait_recv()
    far_up2.wait_recv()
    far_down2.wait_recv()

    @pl.loop(0, QUART // 64)
    def _(n):
        rows = pl.ds(pl.multiple_of(n * 64, 64), 64)
        v = scales[0] * g_own[rows, :]
        for k in (1, 2, 3):
            v += scales[k] * g_recv[k, rows, :].astype(F32)
        for k in range(N):
            v += d_recv[k, rows, :].astype(F32)
        v = v * (1.0 / N)
        part[1] += folded(v * v)
        avg_all[0, rows, :] = v.astype(avg_all.dtype)

    up = push(avg_all.at[0], avg_all.at[3], at_x(1))
    down = push(avg_all.at[0], avg_all.at[1], at_x(3))
    outs = [fetch(avg_all.at[0], avg_ref.at[x])]
    b = group_sum(part[1])
    sq_ref[...] = summed(gathered(b, ring(at_x)))
    up.wait_recv()
    up2 = push(avg_all.at[3, top], avg_all.at[2, top], at_x(1))
    outs.append(fetch(avg_all.at[3], avg_ref.at[lax.rem(x + 3, N)]))
    down.wait_recv()
    down2 = push(avg_all.at[1, low], avg_all.at[2, low], at_x(3))
    outs.append(fetch(avg_all.at[1], avg_ref.at[lax.rem(x + 1, N)]))
    up2.wait_recv()
    down2.wait_recv()
    outs.append(fetch(avg_all.at[2], avg_ref.at[lax.rem(x + 2, N)]))
    for copy in started:
        copy.wait_send()
    for copy in outs:
        copy.wait()


def averaged(tokens, token_grads, table, gate_weight, down_weight, drift):
    vm = pltpu.VMEM
    dma = pltpu.SemaphoreType.DMA
    return pl.pallas_call(
        kernel,
        out_shape=(
            jax.ShapeDtypeStruct((N, QUART, HID), AVG),
            jax.ShapeDtypeStruct((8, 128), F32),
        ),
        in_specs=[pl.BlockSpec(memory_space=pl.ANY)] * 6,
        out_specs=(pl.BlockSpec(memory_space=pl.ANY), pl.BlockSpec(memory_space=pltpu.VMEM)),
        scratch_shapes=[
            vm((N, TOK, HALF), BF16),
            vm((N, TOK, HALF), BF16),
            vm((N, CAP, 128), F32),
            vm((N, CAP, 128), F32),
            vm((3, N, CAP, HALF), BF16),
            vm((3, N, CAP, HALF), BF16),
            vm((N, CAP, HALF), BF16),
            vm((N, CAP, HALF), BF16),
            vm((2, N, N, CAP, HALF), BF16),
            vm((2, N, N, CAP, HALF), BF16),
            vm((2, HALF, HID), BF16),
            vm((2, HID, HALF), BF16),
            vm((N, GROUP, HID), F32),
            vm((N, GROUP, HID), F32),
            vm((FEAT, ROWS), BF16),
            vm((ROWS, HID), BF16),
            vm((QUART, HID), F32),
            vm((3, QUART, HID), BF16),
            vm((2, QUART // 2, HID), BF16),
            vm((N, QUART, HID), BF16),
            vm((N, QUART, HID), BF16),
            vm((N, QUART, HID), AVG),
            vm((2, 8, 128), F32),
            vm((32, 8, 128), F32),
            dma((128,)),
            dma((128,)),
            dma((16,)),
        ],
        compiler_params=pltpu.CompilerParams(
            collective_id=0, has_side_effects=True, vmem_limit_bytes=67043328
        ),
        name="averaged",
    )(tokens, token_grads, table, gate_weight, down_weight, drift)


def body(
    tokens,
    token_grads,
    slot_token,
    slot_count,
    slot_prob,
    gate_weight,
    down_weight,
    drift,
    momentum,
):
    index = slot_token[0, 0].T
    live = lax.broadcasted_iota(jnp.int32, index.shape, 0) < slot_count[0, 0][None, :]
    index = jnp.where(live, index.astype(F32), -1.0)
    prob = jnp.where(live, slot_prob[0, 0].T, 0.0)
    table = jnp.concatenate([index, prob, jnp.zeros((CAP, 96), F32)], axis=1)
    average, squares = averaged(
        tokens[0], token_grads[0], table, gate_weight[0, 0], down_weight[0, 0], drift[0, 0]
    )
    average = average.reshape(momentum.shape).astype(F32)
    clip_scale = jnp.minimum(1.0, 0.25 * math.sqrt(ENTRIES) / jnp.sqrt(jnp.sum(squares) + 1e-06))
    clipped = clip_scale * average
    new_moment = 0.9 * momentum + clipped
    return (new_moment, (0.7 * (clipped + 0.9 * new_moment)).astype(BF16))


def solution(mesh):
    return jax.shard_map(
        body,
        mesh=mesh,
        in_specs=(
            P("island", "expert", "tensor"),
            P("island", "expert", "tensor"),
            P("island", "expert", None, None),
            P("island", "expert", None),
            P("island", "expert", None, None),
            P("island", "expert", None, "tensor"),
            P("island", "expert", "tensor", None),
            P("island", "expert", None, "tensor"),
            P("expert", None, "tensor"),
        ),
        out_specs=(P("expert", None, "tensor"), P("expert", None, "tensor")),
        check_vma=False,
    )
```

```python
import functools
import math

import jax
import jax.numpy as jnp
from jax import lax
from jax.experimental import pallas as pl
from jax.experimental.pallas import tpu as pltpu
from jax.sharding import PartitionSpec as P

MESH = pl.DeviceIdType.MESH
BF16 = jnp.bfloat16
F32 = jnp.float32
AVG = jnp.bfloat16
N = 4
CAP = 96
GROUP = N * CAP
ROWS = N * GROUP
TOK = 256
HALF = 1024
FEAT = 2 * HALF
QUART = FEAT // N
HID = 768
TILE = 256
COLS = 256
GCOLS = 256
PIECES = 2
LAST = 256
ENTRIES = 16 * 2048 * 1536


def back(k):
    return (N - k) % N


class Sent:
    def __init__(self, copy):
        self.copy, self.arrived = copy, False

    def wait(self):
        if not self.arrived:
            self.copy.wait()
        self.arrived = True

    def wait_recv(self):
        if not self.arrived:
            self.copy.wait_recv()
        self.arrived = True

    def wait_send(self):
        self.copy.wait_send()


def kernel(
    tok_ref, tg_ref, slot_ref, count_ref, prob_ref, wg_ref, wd_ref, drift_ref,
    avg_ref, scale_ref,
    tok_z, tg_y, tab_z, tab_y, send_x, send_g, relay_x, relay_g, xs, gs, wg, wd,
    gate, backg, xt, hid, g_own, g_far, g_near, g_mine, g_join, g_relay, g_direct, g_recv, d_recv, avg_all,
    part, tiles, slots, counts, probs, table, send_sem, recv_sem, local_sem,
):
    x = lax.axis_index("island")
    ex = lax.axis_index("expert")
    t = lax.axis_index("tensor")
    z, y = ex // N, lax.rem(ex, N)

    def at_x(k):
        return {"island": lax.rem(x + k, N)}

    def at_z(k):
        return {"expert": lax.rem(z + k, N) * N + y}

    def at_y(k):
        return {"expert": z * N + lax.rem(y + k, N)}

    partner = {"tensor": 1 - t}
    started, fetched = [], []

    def push(src, dst, device):
        i = len(started)
        copy = pltpu.make_async_remote_copy(
            src_ref=src, dst_ref=dst, send_sem=send_sem.at[i], recv_sem=recv_sem.at[i],
            device_id=device, device_id_type=MESH,
        )
        copy.start()
        started.append(Sent(copy))
        return started[-1]

    def fetch(src, dst):
        copy = pltpu.make_async_copy(src, dst, local_sem.at[len(fetched)])
        copy.start()
        fetched.append(Sent(copy))
        return fetched[-1]

    own_slots = [fetch(slot_ref, slots), fetch(count_ref, counts), fetch(prob_ref, probs)]
    own_tok = fetch(tok_ref, tok_z.at[0])
    own_tg = fetch(tg_ref, tg_y.at[0])
    mine, theirs = pl.ds(0, HALF), pl.ds(HALF, HALF)
    own_half = pl.ds(pl.multiple_of(t * HALF, HALF), HALF)
    other_half = pl.ds(pl.multiple_of((1 - t) * HALF, HALF), HALF)
    loads = [
        fetch(wg_ref.at[own_half, :], wg.at[mine, :]),
        fetch(wg_ref.at[other_half, :], wg.at[theirs, :]),
        fetch(wd_ref.at[:, own_half], wd.at[:, mine]),
        fetch(wd_ref.at[:, other_half], wd.at[:, theirs]),
    ]

    def quarter(k):
        return pl.ds(pl.multiple_of(lax.rem(x + k, N) * QUART, QUART), QUART)

    own_drift = fetch(drift_ref.at[quarter(0), :], d_recv.at[0])

    barrier = pltpu.get_barrier_semaphore()
    peers = [at(k) for at in (at_x, at_y, at_z) for k in (1, 2, 3)] + [partner]
    for peer in peers:
        pl.semaphore_signal(barrier, inc=1, device_id=peer, device_id_type=MESH)
    pl.semaphore_wait(barrier, len(peers))

    tok_up = push(tok_ref, tok_z.at[3], at_z(1))
    tok_down = push(tok_ref, tok_z.at[1], at_z(3))
    tg_up = push(tg_ref, tg_y.at[3], at_y(1))
    tg_down = push(tg_ref, tg_y.at[1], at_y(3))
    for copy in own_slots:
        copy.wait()
    alive = lax.broadcasted_iota(jnp.int32, (CAP, 16), 0) < counts[...]
    table[...] = jnp.zeros_like(table)
    table[:, 0:16] = jnp.where(alive, slots[...].astype(F32).T, -1.0)
    table[:, 16:32] = jnp.where(alive, probs[...].T, 0.0)
    tz = {k: push(table, tab_z.at[back(k)], at_z(k)) for k in (1, 3, 2)}
    ty = {k: push(table, tab_y.at[back(k)], at_y(k)) for k in (1, 3, 2)}
    drifts = [push(drift_ref.at[quarter(k), :], d_recv.at[back(k)], at_x(k)) for k in (2, 1, 3)]

    lane = lax.broadcasted_iota(jnp.int32, (CAP, 128), 1)
    token_of = lax.broadcasted_iota(jnp.int32, (CAP, TOK), 1).astype(F32)

    def column(tab, at):
        return jnp.sum(jnp.where(lane == at, tab, 0.0), axis=1, keepdims=True)

    def picked(tab, rows, expert, weighted):
        chosen = jnp.where(column(tab, expert) == token_of, 1.0, 0.0).astype(BF16)
        out = jnp.dot(chosen, rows, preferred_element_type=F32)
        if weighted:
            out = out * column(tab, expert + 16)
        return out.astype(BF16)

    chunk = {}
    relays = {}

    def scatter_x(kz):
        tab, rows = (tab_z[kz] if kz else table[...]), tok_z[kz]
        for ky in (2, 1, 3, 0):
            expert = z * N + lax.rem(y + ky, N)
            got = picked(tab, rows, expert, False)
            if ky == 0:
                xs[kz, 0, :, :HALF] = got
                continue
            send_x[ky - 1, kz] = got
            src = send_x.at[ky - 1, kz]
            if ky == 2:
                way = 1 if kz in (0, 2) else 3
                relays["x", kz] = (push(src, relay_x.at[kz], at_y(way)), way)
            else:
                chunk["x", kz, back(ky)] = push(src, xs.at[kz, back(ky), :, mine], at_y(ky))

    def scatter_g(ky):
        tab, rows = (tab_y[ky] if ky else table[...]), tg_y[ky]
        for kz in (2, 1, 3, 0):
            expert = lax.rem(z + kz, N) * N + y
            got = picked(tab, rows, expert, True)
            if kz == 0:
                gs[ky, 0, :, :HALF] = got
                continue
            send_g[kz - 1, ky] = got
            src = send_g.at[kz - 1, ky]
            if kz == 2:
                way = 1 if ky in (0, 2) else 3
                relays["g", ky] = (push(src, relay_g.at[ky], at_z(way)), way)
            else:
                chunk["g", ky, back(kz)] = push(src, gs.at[ky, back(kz), :, mine], at_z(kz))

    shared = {}

    def finish():
        for copy in started:
            copy.wait_recv()
            copy.wait_send()
        for copy in fetched:
            copy.wait()

    def share(name, group, member):
        if member:
            chunk[name, group, member].wait_recv()
        buf = xs if name == "x" else gs
        shared[name, group, member] = push(
            buf.at[group, member, :, mine], buf.at[group, member, :, theirs], partner
        )

    def relay(name, group):
        copy, way = relays[name, group]
        copy.wait_recv()
        if name == "x":
            chunk[name, group, 2] = push(relay_x.at[group], xs.at[group, 2, :, mine], at_y(way))
        else:
            chunk[name, group, 2] = push(relay_g.at[group], gs.at[group, 2, :, mine], at_z(way))

    def gate_group(kz):
        for m in range(N):
            shared["x", kz, m].wait_recv()

        @pl.loop(0, HID // COLS)
        def _(n):
            cols = pl.ds(pl.multiple_of(n * COLS, COLS), COLS)
            v = jnp.dot(xs[kz].reshape(GROUP, FEAT), wg[:, cols], preferred_element_type=F32)
            gate[kz, :, cols] = v / (1.0 + jnp.exp(-v))

        @pl.loop(0, FEAT // TILE)
        def _(n):
            cols = pl.ds(pl.multiple_of(n * TILE, TILE), TILE)
            xt[cols, kz * GROUP : (kz + 1) * GROUP] = xs[kz, :, :, cols].reshape(GROUP, TILE).T

    nt = (((1,), (1,)), ((), ()))

    def back_group(ky):
        for m in range(N):
            shared["g", ky, m].wait_recv()

        @pl.loop(0, HID // COLS)
        def _(n):
            cols = pl.ds(pl.multiple_of(n * COLS, COLS), COLS)
            v = lax.dot_general(
                gs[ky].reshape(GROUP, FEAT), wd[cols, :], nt, preferred_element_type=F32
            )
            backg[ky, :, cols] = v

    def hidden(kz, ky):
        rows = slice(kz * GROUP + ky * CAP, kz * GROUP + (ky + 1) * CAP)
        hid[rows, :] = (backg[ky, kz * CAP : (kz + 1) * CAP, :] * gate[kz, ky * CAP : (ky + 1) * CAP, :]).astype(BF16)

    own_tok.wait()
    scatter_x(0)
    own_tg.wait()
    scatter_g(0)
    share("x", 0, 0)
    share("g", 0, 0)

    tok_up.wait_recv()
    tok_relay_up = push(tok_z.at[3, pl.ds(0, TOK // 2)], tok_z.at[2, pl.ds(0, TOK // 2)], at_z(1))
    tg_up.wait_recv()
    tg_relay_up = push(tg_y.at[3, pl.ds(0, TOK // 2)], tg_y.at[2, pl.ds(0, TOK // 2)], at_y(1))
    tok_down.wait_recv()
    tok_relay_down = push(
        tok_z.at[1, pl.ds(TOK // 2, TOK // 2)], tok_z.at[2, pl.ds(TOK // 2, TOK // 2)], at_z(3)
    )
    tg_down.wait_recv()
    tg_relay_down = push(
        tg_y.at[1, pl.ds(TOK // 2, TOK // 2)], tg_y.at[2, pl.ds(TOK // 2, TOK // 2)], at_y(3)
    )
    for k in (3, 1):
        tz[back(k)].wait_recv()
        scatter_x(k)
        ty[back(k)].wait_recv()
        scatter_g(k)
        share("x", k, 0)
        share("g", k, 0)
    relay("x", 0)
    relay("g", 0)
    for m in (1, 3):
        share("x", 0, m)
        share("g", 0, m)
    for k in (3, 1):
        relay("x", k)
        relay("g", k)
    tok_relay_up.wait_recv()
    tok_relay_down.wait_recv()
    tz[2].wait_recv()
    scatter_x(2)
    tg_relay_up.wait_recv()
    tg_relay_down.wait_recv()
    ty[2].wait_recv()
    scatter_g(2)
    share("x", 0, 2)
    share("g", 0, 2)
    share("x", 2, 0)
    share("g", 2, 0)
    for k in (3, 1):
        for m in (1, 3):
            share("x", k, m)
            share("g", k, m)
    for load in loads:
        load.wait()
    gate_group(0)
    back_group(0)
    hidden(0, 0)
    for k in (3, 1):
        share("x", k, 2)
        share("g", k, 2)
    relay("x", 2)
    relay("g", 2)
    for k in (3, 1):
        gate_group(k)
        back_group(k)
    for kz in (0, 1, 3):
        for ky in (0, 1, 3):
            if kz or ky:
                hidden(kz, ky)
    for m in (1, 3, 2):
        share("x", 2, m)
        share("g", 2, m)
    gate_group(2)
    back_group(2)
    for k in (0, 1, 3):
        hidden(2, k)
        hidden(k, 2)
    hidden(2, 2)

    part[...] = jnp.zeros_like(part)

    def folded(v):
        s = jnp.sum(v.reshape(v.shape[0] // 8, 8, v.shape[1]), axis=0)
        return sum(s[:, i * 128 : (i + 1) * 128] for i in range(v.shape[1] // 128))

    def gradient(k, store):
        d = lax.rem(x + k, N)
        at = lax.rem(d // 2 + t, 2) * HALF + lax.rem(d, 2) * QUART
        rows = pl.ds(pl.multiple_of(at, QUART), QUART)

        @pl.loop(0, HID // GCOLS)
        def _(n):
            cols = pl.ds(pl.multiple_of(n * GCOLS, GCOLS), GCOLS)
            v = jnp.dot(xt[rows, :], hid[:, cols], preferred_element_type=F32)
            part[0] += folded(v * v)
            store(cols, v)

    top, low = pl.ds(0, QUART // 2), pl.ds(QUART // 2, QUART // 2)

    def far(cols, v):
        g_far[:, cols] = v.astype(BF16)

    def up_side(cols, v):
        g_mine[0, :, cols] = v[: QUART // 2]
        g_near[0, :, cols] = v[QUART // 2 :].astype(BF16)

    def down_side(cols, v):
        g_near[1, :, cols] = v[: QUART // 2].astype(BF16)
        g_mine[1, :, cols] = v[QUART // 2 :]

    def keeping(cols, v):
        g_own[:, cols] = v

    gradient(2, far)
    far_up = push(g_far.at[top], g_relay.at[0], at_x(1))
    far_down = push(g_far.at[low], g_relay.at[1], at_x(3))
    gradient(1, up_side)
    near_up = push(g_near.at[0], g_direct.at[1], at_x(1))
    gradient(3, down_side)
    near_down = push(g_near.at[1], g_direct.at[0], at_x(3))
    gradient(0, keeping)

    slot = [0]

    def gathered(value, pushes):
        first = slot[0]
        slot[0] += 1 + len(pushes)
        tiles[first] = value
        copies = []
        for i, (device, place) in enumerate(pushes):
            copies.append(push(tiles.at[first], tiles.at[first + place], device))
        for copy in copies:
            copy.wait_recv()
        return [tiles[first + i] for i in range(1 + len(pushes))]

    def ring(at):
        return [(at(k), back(k)) for k in (1, 2, 3)]

    def summed(v):
        return (v[0] + v[2]) + (v[1] + v[3])

    def group_sum(value):
        a = gathered(value, [(partner, 1)])
        b = summed(gathered(a[0] + a[1], ring(at_z)))
        return summed(gathered(b, ring(at_y)))

    square = group_sum(part[0])
    squares = gathered(square, ring(at_x))
    scales = []
    for v in squares:
        total = jnp.sum(jnp.sum(v, axis=1, keepdims=True), axis=0, keepdims=True)
        scales.append(jnp.minimum(1.0, math.sqrt(ENTRIES) / jnp.sqrt(total + 1e-06)))

    piece = QUART // 2 // PIECES
    joined = []
    for copy in (far_up, far_down):
        copy.wait_recv()
    for p in range(PIECES):
        rows = pl.ds(p * piece, piece)
        for side, way in ((0, 1), (1, 3)):
            from_there = scales[back(way)] * g_relay[side, rows, :].astype(F32)
            g_join[side, rows, :] = (from_there + scales[0] * g_mine[side, rows, :]).astype(BF16)
            joined.append(push(g_join.at[side, rows], g_recv.at[side, rows], at_x(way)))

    own_drift.wait()
    for copy in drifts:
        copy.wait_recv()
    near_up.wait_recv()
    near_down.wait_recv()

    ups, downs = {}, {}
    for p in range(PIECES):
        for side in range(2):
            joined[2 * p + side].wait_recv()
            direct = scales[1] if side == 0 else scales[3]

            @pl.loop(0, piece // 64)
            def _(n):
                at = pl.multiple_of(p * piece + n * 64, 64)
                near = pl.ds(at, 64)
                rows = pl.ds(pl.multiple_of(side * (QUART // 2) + at, 64), 64)
                v = scales[0] * g_own[rows, :]
                v += direct * g_direct[side, near, :].astype(F32)
                v += g_recv[side, near, :].astype(F32)
                for k in range(N):
                    v += d_recv[k, rows, :].astype(F32)
                v = v * (1.0 / N)
                part[1] += folded(v * v)
                avg_all[0, rows, :] = v.astype(avg_all.dtype)

        at = {side: pl.ds(side * (QUART // 2) + p * piece, piece) for side in range(2)}
        for side in (0, 1):
            ups[p, side] = push(avg_all.at[0, at[side]], avg_all.at[3, at[side]], at_x(1))
        for side in (1, 0):
            downs[p, side] = push(avg_all.at[0, at[side]], avg_all.at[1, at[side]], at_x(3))

    fetch(avg_all.at[0], avg_ref.at[quarter(0), :])
    passed = []

    def pass_on(p):
        rows = pl.ds(p * piece, piece)
        ups[p, 0].wait_recv()
        passed.append(push(avg_all.at[3, rows], avg_all.at[2, rows], at_x(1)))
        rows = pl.ds(QUART // 2 + p * piece, piece)
        downs[p, 1].wait_recv()
        passed.append(push(avg_all.at[1, rows], avg_all.at[2, rows], at_x(3)))

    pass_on(0)
    b = group_sum(part[1])
    total = summed(gathered(b, ring(at_x)))
    total = jnp.sum(jnp.sum(total, axis=1, keepdims=True), axis=0, keepdims=True)
    scale = jnp.minimum(1.0, 0.25 * math.sqrt(ENTRIES) / jnp.sqrt(total + 1e-06))
    scale_ref[...] = jnp.broadcast_to(scale, scale_ref.shape)
    for p in range(1, PIECES):
        pass_on(p)
    for p in range(PIECES):
        ups[p, 1].wait_recv()
        downs[p, 0].wait_recv()
    fetch(avg_all.at[3], avg_ref.at[quarter(3), :])
    fetch(avg_all.at[1], avg_ref.at[quarter(1), :])
    for copy in passed:
        copy.wait_recv()
    fetch(avg_all.at[2], avg_ref.at[quarter(2), :])
    finish()


def averaged(tokens, token_grads, slots, counts, probs, gate_weight, down_weight, drift):
    vm = pltpu.VMEM
    dma = pltpu.SemaphoreType.DMA
    return pl.pallas_call(
        kernel,
        out_shape=(
            jax.ShapeDtypeStruct((FEAT, HID), AVG),
            jax.ShapeDtypeStruct((8, 128), F32),
        ),
        in_specs=[pl.BlockSpec(memory_space=pl.ANY)] * 8,
        out_specs=(pl.BlockSpec(memory_space=pl.ANY), pl.BlockSpec(memory_space=pltpu.VMEM)),
        scratch_shapes=[
            vm((N, TOK, HALF), BF16),
            vm((N, TOK, HALF), BF16),
            vm((N, CAP, 128), F32),
            vm((N, CAP, 128), F32),
            vm((3, N, CAP, HALF), BF16),
            vm((3, N, CAP, HALF), BF16),
            vm((N, CAP, HALF), BF16),
            vm((N, CAP, HALF), BF16),
            vm((N, N, CAP, FEAT), BF16),
            vm((N, N, CAP, FEAT), BF16),
            vm((FEAT, HID), BF16),
            vm((HID, FEAT), BF16),
            vm((N, GROUP, HID), F32),
            vm((N, GROUP, HID), F32),
            vm((FEAT, ROWS), BF16),
            vm((ROWS, HID), BF16),
            vm((QUART, HID), F32),
            vm((QUART, HID), BF16),
            vm((2, QUART // 2, HID), BF16),
            vm((2, QUART // 2, HID), F32),
            vm((2, QUART // 2, HID), BF16),
            vm((2, QUART // 2, HID), BF16),
            vm((2, QUART // 2, HID), BF16),
            vm((2, QUART // 2, HID), BF16),
            vm((N, QUART, HID), BF16),
            vm((N, QUART, HID), AVG),
            vm((2, 8, 128), F32),
            vm((32, 8, 128), F32),
            vm((16, CAP), jnp.int32),
            vm((1, 16), jnp.int32),
            vm((16, CAP), F32),
            vm((CAP, 128), F32),
            dma((160,)),
            dma((160,)),
            dma((16,)),
        ],
        compiler_params=pltpu.CompilerParams(
            collective_id=0, has_side_effects=True, vmem_limit_bytes=67043328
        ),
        name="averaged",
    )(tokens, token_grads, slots, counts, probs, gate_weight, down_weight, drift)


def last(scale_ref, avg_ref, old_ref, new_ref, step_ref):
    clipped = scale_ref[0, 0] * avg_ref[...].astype(F32)
    new = 0.9 * old_ref[...] + clipped
    new_ref[...] = new
    step_ref[...] = (0.7 * (clipped + 0.9 * new)).astype(BF16)


def updated(scale, average, momentum):
    block = pl.BlockSpec((LAST, HID), lambda i: (i, 0))
    return pl.pallas_call(
        last,
        grid=(FEAT // LAST,),
        out_shape=(
            jax.ShapeDtypeStruct((FEAT, HID), F32),
            jax.ShapeDtypeStruct((FEAT, HID), BF16),
        ),
        in_specs=[pl.BlockSpec(memory_space=pltpu.SMEM), block, block],
        out_specs=(block, block),
        compiler_params=pltpu.CompilerParams(vmem_limit_bytes=67043328),
        name="updated",
    )(scale, average, momentum)


def body(
    tokens,
    token_grads,
    slot_token,
    slot_count,
    slot_prob,
    gate_weight,
    down_weight,
    drift,
    momentum,
):
    average, scale = averaged(
        tokens[0], token_grads[0], slot_token[0, 0], slot_count[0], slot_prob[0, 0],
        gate_weight[0, 0], down_weight[0, 0], drift[0, 0],
    )
    new_momentum, outer_step = updated(scale, average, momentum[0])
    return (new_momentum[None], outer_step[None])


def solution(mesh):
    return jax.shard_map(
        body,
        mesh=mesh,
        in_specs=(
            P("island", "expert", "tensor"),
            P("island", "expert", "tensor"),
            P("island", "expert", None, None),
            P("island", "expert", None),
            P("island", "expert", None, None),
            P("island", "expert", None, "tensor"),
            P("island", "expert", "tensor", None),
            P("island", "expert", None, "tensor"),
            P("expert", None, "tensor"),
        ),
        out_specs=(P("expert", None, "tensor"), P("expert", None, "tensor")),
        check_vma=False,
    )
```

```python
import functools
import math

import jax
import jax.numpy as jnp
from jax import lax
from jax.experimental import pallas as pl
from jax.experimental.pallas import tpu as pltpu
from jax.sharding import PartitionSpec as P

MESH = pl.DeviceIdType.MESH
BF16 = jnp.bfloat16
F32 = jnp.float32
AVG = jnp.bfloat16
N = 4
CAP = 96
GROUP = N * CAP
ROWS = N * GROUP
TOK = 256
HALF = 1024
FEAT = 2 * HALF
QUART = FEAT // N
HID = 768
TILE = 256
COLS = 256
GCOLS = 256
PIECES = 2
VMEM_AVERAGED = 55 << 20
VMEM_UPDATED = 57 << 20
WAY = (1, 3, 1, 3)
PLACE = (0, 1, 3, 2)
SENDS = 56
COPIES = 107
LAST = 256
ENTRIES = 16 * 2048 * 1536


def back(k):
    return (N - k) % N


class Sent:
    def __init__(self, copy):
        self.copy, self.arrived, self.sent = copy, False, False

    def wait(self):
        if not self.arrived:
            self.copy.wait()
        self.arrived = True

    def wait_recv(self):
        if not self.arrived:
            self.copy.wait_recv()
        self.arrived = True

    def wait_send(self):
        if not self.sent:
            self.copy.wait_send()
        self.sent = True


def kernel(
    tok_ref, tg_ref, slot_ref, count_ref, prob_ref, wg_ref, wd_ref, drift_ref,
    avg_ref, scale_ref,
    tok_z, tg_y, tab_z, tab_y, send_x, send_g, relay_x, relay_g, xs, gs, wg, wd,
    gate, backg, xt, hid, g_relay, g_direct, g_recv, d_recv, avg_all,
    part, tiles, slots, counts, probs, table, send_sem, recv_sem, local_sem,
):
    x = lax.axis_index("island")
    ex = lax.axis_index("expert")
    t = lax.axis_index("tensor")
    z, y = ex // N, lax.rem(ex, N)

    def at_x(k):
        return {"island": lax.rem(x + k, N)}

    def at_z(k):
        return {"expert": lax.rem(z + k, N) * N + y}

    def at_y(k):
        return {"expert": z * N + lax.rem(y + k, N)}

    partner = {"tensor": 1 - t}
    started, fetched = [], []

    def push(src, dst, device):
        i = len(started)
        if i >= SENDS:
            started[i - SENDS].wait_send()
        copy = pltpu.make_async_remote_copy(
            src_ref=src, dst_ref=dst, send_sem=send_sem.at[i % SENDS], recv_sem=recv_sem.at[i],
            device_id=device, device_id_type=MESH,
        )
        copy.start()
        started.append(Sent(copy))
        return started[-1]

    def fetch(src, dst):
        copy = pltpu.make_async_copy(src, dst, local_sem.at[len(fetched)])
        copy.start()
        fetched.append(Sent(copy))
        return fetched[-1]

    own_slots = [fetch(slot_ref, slots), fetch(count_ref, counts), fetch(prob_ref, probs)]
    own_tok = fetch(tok_ref, tok_z.at[0])
    own_tg = fetch(tg_ref, tg_y.at[0])
    mine, theirs = pl.ds(0, HALF), pl.ds(HALF, HALF)
    own_half = pl.ds(pl.multiple_of(t * HALF, HALF), HALF)
    other_half = pl.ds(pl.multiple_of((1 - t) * HALF, HALF), HALF)
    loads = [
        fetch(wg_ref.at[own_half, :], wg.at[mine, :]),
        fetch(wg_ref.at[other_half, :], wg.at[theirs, :]),
        fetch(wd_ref.at[:, own_half], wd.at[:, mine]),
        fetch(wd_ref.at[:, other_half], wd.at[:, theirs]),
    ]

    def quarter(k):
        return pl.ds(pl.multiple_of(lax.rem(x + k, N) * QUART, QUART), QUART)

    own_drift = fetch(drift_ref.at[quarter(0), :], d_recv.at[0])

    barrier = pltpu.get_barrier_semaphore()
    peers = [at(k) for at in (at_x, at_y, at_z) for k in (1, 2, 3)] + [partner]
    for peer in peers:
        pl.semaphore_signal(barrier, inc=1, device_id=peer, device_id_type=MESH)
    pl.semaphore_wait(barrier, len(peers))

    tok_up = push(tok_ref, tok_z.at[3], at_z(1))
    tok_down = push(tok_ref, tok_z.at[1], at_z(3))
    tg_up = push(tg_ref, tg_y.at[3], at_y(1))
    tg_down = push(tg_ref, tg_y.at[1], at_y(3))
    for copy in own_slots:
        copy.wait()
    across = lax.broadcasted_iota(jnp.int32, (16, 16), 1)
    diagonal = lax.broadcasted_iota(jnp.int32, (16, 16), 0) == across
    filled = jnp.sum(jnp.where(diagonal, counts[...], 0), axis=1, keepdims=True)
    alive = lax.broadcasted_iota(jnp.int32, (16, CAP), 1) < filled
    table[...] = jnp.zeros_like(table)
    table[0:16, 0:CAP] = jnp.where(alive, slots[...].astype(F32), -1.0)
    table[16:32, 0:CAP] = jnp.where(alive, probs[...], 0.0)
    names = pl.ds(0, 16)
    tz = {k: push(table.at[names], tab_z.at[back(k), names], at_z(k)) for k in (1, 3, 2)}
    ty = {k: push(table, tab_y.at[back(k)], at_y(k)) for k in (1, 3, 2)}
    drifts = [push(drift_ref.at[quarter(k), :], d_recv.at[back(k)], at_x(k)) for k in (2, 1, 3)]

    lane = lax.broadcasted_iota(jnp.int32, (CAP, 32), 1)
    token_of = lax.broadcasted_iota(jnp.int32, (CAP, TOK), 1).astype(F32)

    def column(tab, at):
        return jnp.sum(jnp.where(lane == at, tab, 0.0), axis=1, keepdims=True)

    def picked(tab, rows, expert, weighted):
        chosen = jnp.where(column(tab, expert) == token_of, 1.0, 0.0).astype(BF16)
        out = jnp.dot(chosen, rows, preferred_element_type=F32)
        if weighted:
            out = out * column(tab, expert + 16)
        return out.astype(BF16)

    chunk = {}
    relays = {}

    def scatter_x(kz):
        tab, rows = (tab_z[kz] if kz else table[...]).T[:CAP], tok_z[kz]
        for ky in (2, 1, 3, 0):
            expert = z * N + lax.rem(y + ky, N)
            got = picked(tab, rows, expert, False)
            if ky == 0:
                xs[kz, 0, :, :HALF] = got
                continue
            send_x[ky - 1, kz] = got
            src = send_x.at[ky - 1, kz]
            if ky == 2:
                relays["x", kz] = push(src, relay_x.at[kz], at_y(WAY[kz]))
            else:
                chunk["x", kz, back(ky)] = push(src, xs.at[kz, PLACE[back(ky)], :, mine], at_y(ky))

    def scatter_g(ky):
        tab, rows = (tab_y[ky] if ky else table[...]).T[:CAP], tg_y[ky]
        for kz in (2, 1, 3, 0):
            expert = lax.rem(z + kz, N) * N + y
            got = picked(tab, rows, expert, True)
            if kz == 0:
                gs[ky, 0, :, :HALF] = got
                continue
            send_g[kz - 1, ky] = got
            src = send_g.at[kz - 1, ky]
            if kz == 2:
                relays["g", ky] = push(src, relay_g.at[ky], at_z(WAY[ky]))
            else:
                chunk["g", ky, back(kz)] = push(src, gs.at[ky, PLACE[back(kz)], :, mine], at_z(kz))

    shared = {}

    def finish():
        for copy in started:
            copy.wait_recv()
            copy.wait_send()
        for copy in fetched:
            copy.wait()

    def share(name, group, members):
        for member in members:
            if member:
                chunk[name, group, member].wait_recv()
        buf = xs if name == "x" else gs
        places = pl.ds(PLACE[members[0]], len(members))
        shared.setdefault((name, group), []).append(
            push(buf.at[group, places, :, mine], buf.at[group, places, :, theirs], partner)
        )

    def relay(name, group):
        held, buf, at = (relay_x, xs, at_y) if name == "x" else (relay_g, gs, at_z)
        relays[name, group].wait_recv()
        chunk[name, group, 2] = push(
            held.at[group], buf.at[group, PLACE[2], :, mine], at(WAY[group])
        )

    def gate_group(kz):
        for copy in shared["x", kz]:
            copy.wait_recv()

        @pl.loop(0, HID // COLS)
        def _(n):
            cols = pl.ds(pl.multiple_of(n * COLS, COLS), COLS)
            v = jnp.dot(xs[kz].reshape(GROUP, FEAT), wg[:, cols], preferred_element_type=F32)
            gate[pl.ds(kz * GROUP, GROUP), cols] = v / (1.0 + jnp.exp(-v))

        @pl.loop(0, FEAT // TILE)
        def _(n):
            cols = pl.ds(pl.multiple_of(n * TILE, TILE), TILE)
            xt[cols, kz * GROUP : (kz + 1) * GROUP] = xs[kz, :, :, cols].reshape(GROUP, TILE).T

    nt = (((1,), (1,)), ((), ()))

    def back_group(ky):
        for copy in shared["g", ky]:
            copy.wait_recv()

        @pl.loop(0, HID // COLS)
        def _(n):
            cols = pl.ds(pl.multiple_of(n * COLS, COLS), COLS)
            v = lax.dot_general(
                gs[ky].reshape(GROUP, FEAT), wd[cols, :], nt, preferred_element_type=F32
            )
            backg[pl.ds(ky * GROUP, GROUP), cols] = v

    def hidden(kz, ky):
        rows = pl.ds(kz * GROUP + PLACE[ky] * CAP, CAP)
        others = pl.ds(ky * GROUP + PLACE[kz] * CAP, CAP)
        hid[rows, :] = (backg[others, :] * gate[rows, :]).astype(BF16)

    own_tok.wait()
    scatter_x(0)
    own_tg.wait()
    scatter_g(0)
    tok_up.wait_recv()
    tok_relay_up = push(tok_z.at[3, pl.ds(0, TOK // 2)], tok_z.at[2, pl.ds(0, TOK // 2)], at_z(1))
    tg_up.wait_recv()
    tg_relay_up = push(tg_y.at[3, pl.ds(0, TOK // 2)], tg_y.at[2, pl.ds(0, TOK // 2)], at_y(1))
    tok_down.wait_recv()
    tok_relay_down = push(
        tok_z.at[1, pl.ds(TOK // 2, TOK // 2)], tok_z.at[2, pl.ds(TOK // 2, TOK // 2)], at_z(3)
    )
    tg_down.wait_recv()
    tg_relay_down = push(
        tg_y.at[1, pl.ds(TOK // 2, TOK // 2)], tg_y.at[2, pl.ds(TOK // 2, TOK // 2)], at_y(3)
    )
    for k in (3, 1):
        tz[back(k)].wait_recv()
        scatter_x(k)
        ty[back(k)].wait_recv()
        scatter_g(k)
    relay("x", 0)
    relay("g", 0)
    share("x", 0, (0, 1, 3))
    share("g", 0, (0, 1, 3))
    tok_relay_up.wait_recv()
    tok_relay_down.wait_recv()
    tz[2].wait_recv()
    scatter_x(2)
    tg_relay_up.wait_recv()
    tg_relay_down.wait_recv()
    ty[2].wait_recv()
    scatter_g(2)
    relay("x", 3)
    relay("g", 3)
    share("x", 3, (0, 1, 3))
    share("g", 3, (0, 1, 3))
    relay("x", 1)
    relay("g", 1)
    share("x", 0, (2,))
    share("g", 0, (2,))
    share("x", 1, (0, 1, 3))
    share("g", 1, (0, 1, 3))
    for load in loads:
        load.wait()
    gate_group(0)
    back_group(0)
    hidden(0, 0)
    share("x", 3, (2,))
    share("g", 3, (2,))
    relay("x", 2)
    relay("g", 2)
    gate_group(3)
    back_group(3)
    share("x", 1, (2,))
    share("g", 1, (2,))
    share("x", 2, (0, 1, 3))
    share("g", 2, (0, 1, 3))
    gate_group(1)
    back_group(1)
    for kz in (0, 1, 3):
        for ky in (0, 1, 3):
            if kz or ky:
                hidden(kz, ky)
    share("x", 2, (2,))
    share("g", 2, (2,))
    gate_group(2)
    back_group(2)
    for k in (0, 1, 3):
        hidden(2, k)
        hidden(k, 2)
    hidden(2, 2)

    g_own, g_mine = gate.at[pl.ds(0, QUART)], gate.at[pl.ds(QUART, QUART)]
    g_far, g_near = wg.at[pl.ds(0, QUART)], wg.at[pl.ds(QUART, QUART)]
    g_join = wg.at[pl.ds(2 * QUART, QUART)]
    part[...] = jnp.zeros_like(part)

    def folded(v):
        s = jnp.sum(v.reshape(v.shape[0] // 8, 8, v.shape[1]), axis=0)
        return sum(s[:, i * 128 : (i + 1) * 128] for i in range(v.shape[1] // 128))

    def gradient(k, store):
        d = lax.rem(x + k, N)
        at = lax.rem(d // 2 + t, 2) * HALF + lax.rem(d, 2) * QUART
        rows = pl.ds(pl.multiple_of(at, QUART), QUART)

        @pl.loop(0, HID // GCOLS)
        def _(n):
            cols = pl.ds(pl.multiple_of(n * GCOLS, GCOLS), GCOLS)
            v = jnp.dot(xt[rows, :], hid[:, cols], preferred_element_type=F32)
            part[0] += folded(v * v)
            store(cols, v)

    top, low = pl.ds(0, QUART // 2), pl.ds(QUART // 2, QUART // 2)

    def far(cols, v):
        g_far[:, cols] = v.astype(BF16)

    def up_side(cols, v):
        g_mine[top, cols] = v[: QUART // 2]
        g_near[top, cols] = v[QUART // 2 :].astype(BF16)

    def down_side(cols, v):
        g_near[low, cols] = v[: QUART // 2].astype(BF16)
        g_mine[low, cols] = v[QUART // 2 :]

    def keeping(cols, v):
        g_own[:, cols] = v

    gradient(2, far)
    far_up = push(g_far.at[top], g_relay.at[0], at_x(1))
    far_down = push(g_far.at[low], g_relay.at[1], at_x(3))
    gradient(1, up_side)
    first, second = pl.ds(0, QUART // 4), pl.ds(QUART // 4, QUART // 4)
    near = [push(g_near.at[pl.ds(0, QUART // 4)], g_direct.at[1, first], at_x(1))]
    gradient(3, down_side)
    near.append(push(g_near.at[pl.ds(QUART // 2, QUART // 4)], g_direct.at[0, first], at_x(3)))
    gradient(0, keeping)

    slot = [0]

    def gathered(value, pushes, then=lambda: None):
        first = slot[0]
        slot[0] += 1 + len(pushes)
        tiles[first] = value
        copies = []
        for i, (device, place) in enumerate(pushes):
            copies.append(push(tiles.at[first], tiles.at[first + place], device))
        then()
        for copy in copies:
            copy.wait_recv()
        return [tiles[first + i] for i in range(1 + len(pushes))]

    def ring(at):
        return [(at(k), back(k)) for k in (1, 2, 3)]

    def summed(v):
        return (v[0] + v[2]) + (v[1] + v[3])

    def group_sum(value):
        a = gathered(value, [(partner, 1)])
        b = summed(gathered(a[0] + a[1], ring(at_z)))
        return summed(gathered(b, ring(at_y)))

    def meanwhile():
        near.append(push(g_near.at[pl.ds(QUART // 4, QUART // 4)], g_direct.at[1, second], at_x(1)))
        near.append(push(g_near.at[pl.ds(3 * QUART // 4, QUART // 4)], g_direct.at[0, second], at_x(3)))

    square = group_sum(part[0])
    squares = gathered(square, ring(at_x), meanwhile)
    scales = []
    for v in squares:
        total = jnp.sum(jnp.sum(v, axis=1, keepdims=True), axis=0, keepdims=True)
        scales.append(jnp.minimum(1.0, math.sqrt(ENTRIES) / jnp.sqrt(total + 1e-06)))

    piece = QUART // 2 // PIECES
    joined = []
    for copy in (far_up, far_down):
        copy.wait_recv()
    for p in range(PIECES):
        rows = pl.ds(p * piece, piece)
        for side, way in ((0, 1), (1, 3)):
            from_there = scales[back(way)] * g_relay[side, rows, :].astype(F32)
            both = pl.ds(side * (QUART // 2) + p * piece, piece)
            g_join[both, :] = (from_there + scales[0] * g_mine[both, :]).astype(BF16)
            joined.append(push(g_join.at[both], g_recv.at[side, rows], at_x(way)))

    own_drift.wait()
    for copy in drifts:
        copy.wait_recv()
    for copy in near:
        copy.wait_recv()

    ups, downs = {}, {}
    for p in range(PIECES):
        for side in range(2):
            joined[2 * p + side].wait_recv()
            direct = scales[1] if side == 0 else scales[3]

            @pl.loop(0, piece // 64)
            def _(n):
                at = pl.multiple_of(p * piece + n * 64, 64)
                near = pl.ds(at, 64)
                rows = pl.ds(pl.multiple_of(side * (QUART // 2) + at, 64), 64)
                v = scales[0] * g_own[rows, :]
                v += direct * g_direct[side, near, :].astype(F32)
                v += g_recv[side, near, :].astype(F32)
                for k in range(N):
                    v += d_recv[k, rows, :].astype(F32)
                v = v * (1.0 / N)
                part[1] += folded(v * v)
                avg_all[0, rows, :] = v.astype(avg_all.dtype)

        at = {side: pl.ds(side * (QUART // 2) + p * piece, piece) for side in range(2)}
        for side in (0, 1):
            ups[p, side] = push(avg_all.at[0, at[side]], avg_all.at[3, at[side]], at_x(1))
        for side in (1, 0):
            downs[p, side] = push(avg_all.at[0, at[side]], avg_all.at[1, at[side]], at_x(3))

    fetch(avg_all.at[0], avg_ref.at[quarter(0), :])
    passed = []

    def pass_on(p):
        rows = pl.ds(p * piece, piece)
        ups[p, 0].wait_recv()
        passed.append(push(avg_all.at[3, rows], avg_all.at[2, rows], at_x(1)))
        rows = pl.ds(QUART // 2 + p * piece, piece)
        downs[p, 1].wait_recv()
        passed.append(push(avg_all.at[1, rows], avg_all.at[2, rows], at_x(3)))

    pass_on(0)
    b = group_sum(part[1])
    total = summed(gathered(b, ring(at_x)))
    total = jnp.sum(jnp.sum(total, axis=1, keepdims=True), axis=0, keepdims=True)
    scale = jnp.minimum(1.0, 0.25 * math.sqrt(ENTRIES) / jnp.sqrt(total + 1e-06))
    scale_ref[...] = jnp.broadcast_to(scale, scale_ref.shape)
    for p in range(1, PIECES):
        pass_on(p)
    for p in range(PIECES):
        ups[p, 1].wait_recv()
        downs[p, 0].wait_recv()
    fetch(avg_all.at[3], avg_ref.at[quarter(3), :])
    fetch(avg_all.at[1], avg_ref.at[quarter(1), :])
    for copy in passed:
        copy.wait_recv()
    fetch(avg_all.at[2], avg_ref.at[quarter(2), :])
    finish()


def averaged(tokens, token_grads, slots, counts, probs, gate_weight, down_weight, drift):
    vm = pltpu.VMEM
    dma = pltpu.SemaphoreType.DMA
    return pl.pallas_call(
        kernel,
        out_shape=(
            jax.ShapeDtypeStruct((FEAT, HID), AVG),
            jax.ShapeDtypeStruct((8, 128), F32),
        ),
        in_specs=[pl.BlockSpec(memory_space=pl.ANY)] * 8,
        out_specs=(pl.BlockSpec(memory_space=pl.ANY), pl.BlockSpec(memory_space=pltpu.VMEM)),
        scratch_shapes=[
            vm((N, TOK, HALF), BF16),
            vm((N, TOK, HALF), BF16),
            vm((N, 32, 128), F32),
            vm((N, 32, 128), F32),
            vm((3, N, CAP, HALF), BF16),
            vm((3, N, CAP, HALF), BF16),
            vm((N, CAP, HALF), BF16),
            vm((N, CAP, HALF), BF16),
            vm((N, N, CAP, FEAT), BF16),
            vm((N, N, CAP, FEAT), BF16),
            vm((FEAT, HID), BF16),
            vm((HID, FEAT), BF16),
            vm((ROWS, HID), F32),
            vm((ROWS, HID), F32),
            vm((FEAT, ROWS), BF16),
            vm((ROWS, HID), BF16),
            vm((2, QUART // 2, HID), BF16),
            vm((2, QUART // 2, HID), BF16),
            vm((2, QUART // 2, HID), BF16),
            vm((N, QUART, HID), BF16),
            vm((N, QUART, HID), AVG),
            vm((2, 8, 128), F32),
            vm((32, 8, 128), F32),
            vm((16, CAP), jnp.int32),
            vm((1, 16), jnp.int32),
            vm((16, CAP), F32),
            vm((32, 128), F32),
            dma((SENDS,)),
            dma((COPIES,)),
            dma((14,)),
        ],
        compiler_params=pltpu.CompilerParams(
            collective_id=0, has_side_effects=True, vmem_limit_bytes=VMEM_AVERAGED
        ),
        name="averaged",
    )(tokens, token_grads, slots, counts, probs, gate_weight, down_weight, drift)


def last(scale_ref, avg_ref, old_ref, new_ref, step_ref, avg, new, step, sems):
    copies, reads = [], []
    for i in range(FEAT // LAST):
        rows = pl.ds(i * LAST, LAST)
        reads.append(pltpu.make_async_copy(avg_ref.at[rows], avg.at[rows], sems.at[2, i]))
        reads[-1].start()
    for i in range(FEAT // LAST):
        rows = pl.ds(i * LAST, LAST)
        reads[i].wait()
        clipped = scale_ref[0, 0] * avg[rows, :].astype(F32)
        moment = 0.9 * old_ref[rows, :] + clipped
        new[rows, :] = moment
        step[rows, :] = (0.7 * (clipped + 0.9 * moment)).astype(BF16)
        for j, (src, dst) in enumerate(((new, new_ref), (step, step_ref))):
            copies.append(pltpu.make_async_copy(src.at[rows], dst.at[rows], sems.at[j, i]))
            copies[-1].start()
    for copy in copies:
        copy.wait()


def updated(scale, average, momentum):
    place = pl.BlockSpec(memory_space=pltpu.VMEM)
    out = pl.BlockSpec(memory_space=pl.ANY)
    return pl.pallas_call(
        last,
        out_shape=(
            jax.ShapeDtypeStruct((FEAT, HID), F32),
            jax.ShapeDtypeStruct((FEAT, HID), BF16),
        ),
        in_specs=[pl.BlockSpec(memory_space=pltpu.SMEM), out, place],
        out_specs=(out, out),
        scratch_shapes=[
            pltpu.VMEM((FEAT, HID), AVG),
            pltpu.VMEM((FEAT, HID), F32),
            pltpu.VMEM((FEAT, HID), BF16),
            pltpu.SemaphoreType.DMA((3, FEAT // LAST)),
        ],
        compiler_params=pltpu.CompilerParams(vmem_limit_bytes=VMEM_UPDATED),
        name="updated",
    )(scale, average, momentum)


def body(
    tokens,
    token_grads,
    slot_token,
    slot_count,
    slot_prob,
    gate_weight,
    down_weight,
    drift,
    momentum,
):
    average, scale = averaged(
        tokens[0], token_grads[0], slot_token[0, 0], slot_count[0], slot_prob[0, 0],
        gate_weight[0, 0], down_weight[0, 0], drift[0, 0],
    )
    new_momentum, outer_step = updated(scale, average, momentum[0])
    return (new_momentum[None], outer_step[None])


def solution(mesh):
    return jax.shard_map(
        body,
        mesh=mesh,
        in_specs=(
            P("island", "expert", "tensor"),
            P("island", "expert", "tensor"),
            P("island", "expert", None, None),
            P("island", "expert", None),
            P("island", "expert", None, None),
            P("island", "expert", None, "tensor"),
            P("island", "expert", "tensor", None),
            P("island", "expert", None, "tensor"),
            P("expert", None, "tensor"),
        ),
        out_specs=(P("expert", None, "tensor"), P("expert", None, "tensor")),
        check_vma=False,
    )
```

```python
import functools
import math

import jax
import jax.numpy as jnp
from jax import lax
from jax.experimental import pallas as pl
from jax.experimental.pallas import tpu as pltpu
from jax.sharding import PartitionSpec as P

MESH = pl.DeviceIdType.MESH
BF16 = jnp.bfloat16
F32 = jnp.float32
AVG = jnp.bfloat16
N = 4
CAP = 96
GROUP = N * CAP
ROWS = N * GROUP
TOK = 256
HALF = 1024
FEAT = 2 * HALF
QUART = FEAT // N
HID = 768
TILE = 256
COLS = 256
PIECES = 2
VMEM_AVERAGED = 55 << 20
VMEM_UPDATED = 57 << 20
WAY = (1, 3, 1, 3)
PLACE = (0, 1, 3, 2)
SENDS = 56
COPIES = 111
LAST = 256
ENTRIES = 16 * 2048 * 1536


def back(k):
    return (N - k) % N


class Sent:
    def __init__(self, copy):
        self.copy, self.arrived, self.sent = copy, False, False

    def wait(self):
        if not self.arrived:
            self.copy.wait()
        self.arrived = True

    def wait_recv(self):
        if not self.arrived:
            self.copy.wait_recv()
        self.arrived = True

    def wait_send(self):
        if not self.sent:
            self.copy.wait_send()
        self.sent = True


def kernel(
    tok_ref, tg_ref, slot_ref, count_ref, prob_ref, wg_ref, wd_ref, drift_ref,
    avg_ref, scale_ref,
    tok_z, tg_y, tab_z, tab_y, send_x, send_g, relay_x, relay_g, xs, gs, wg, wd,
    gate, backg, xt, hid, g_relay, g_direct, g_recv, d_recv, avg_all,
    part, tiles, slots, counts, probs, table, send_sem, recv_sem, local_sem,
):
    x = lax.axis_index("island")
    ex = lax.axis_index("expert")
    t = lax.axis_index("tensor")
    z, y = ex // N, lax.rem(ex, N)

    def at_x(k):
        return {"island": lax.rem(x + k, N)}

    def at_z(k):
        return {"expert": lax.rem(z + k, N) * N + y}

    def at_y(k):
        return {"expert": z * N + lax.rem(y + k, N)}

    partner = {"tensor": 1 - t}
    started, fetched = [], []

    def push(src, dst, device):
        i = len(started)
        if i >= SENDS:
            started[i - SENDS].wait_send()
        copy = pltpu.make_async_remote_copy(
            src_ref=src, dst_ref=dst, send_sem=send_sem.at[i % SENDS], recv_sem=recv_sem.at[i],
            device_id=device, device_id_type=MESH,
        )
        copy.start()
        started.append(Sent(copy))
        return started[-1]

    def fetch(src, dst):
        copy = pltpu.make_async_copy(src, dst, local_sem.at[len(fetched)])
        copy.start()
        fetched.append(Sent(copy))
        return fetched[-1]

    own_slots = [fetch(slot_ref, slots), fetch(count_ref, counts), fetch(prob_ref, probs)]
    own_tok = fetch(tok_ref, tok_z.at[0])
    own_tg = fetch(tg_ref, tg_y.at[0])
    mine, theirs = pl.ds(0, HALF), pl.ds(HALF, HALF)
    own_half = pl.ds(pl.multiple_of(t * HALF, HALF), HALF)
    other_half = pl.ds(pl.multiple_of((1 - t) * HALF, HALF), HALF)
    loads = [
        fetch(wg_ref.at[own_half, :], wg.at[mine, :]),
        fetch(wg_ref.at[other_half, :], wg.at[theirs, :]),
        fetch(wd_ref.at[:, own_half], wd.at[:, mine]),
        fetch(wd_ref.at[:, other_half], wd.at[:, theirs]),
    ]

    def quarter(k):
        return pl.ds(pl.multiple_of(lax.rem(x + k, N) * QUART, QUART), QUART)

    own_drift = fetch(drift_ref.at[quarter(0), :], d_recv.at[0])

    barrier = pltpu.get_barrier_semaphore()
    peers = [at(k) for at in (at_x, at_y, at_z) for k in (1, 2, 3)] + [partner]
    for peer in peers:
        pl.semaphore_signal(barrier, inc=1, device_id=peer, device_id_type=MESH)
    pl.semaphore_wait(barrier, len(peers))

    tok_up = push(tok_ref, tok_z.at[3], at_z(1))
    tok_down = push(tok_ref, tok_z.at[1], at_z(3))
    tg_up = push(tg_ref, tg_y.at[3], at_y(1))
    tg_down = push(tg_ref, tg_y.at[1], at_y(3))
    for copy in own_slots:
        copy.wait()
    across = lax.broadcasted_iota(jnp.int32, (16, 16), 1)
    diagonal = lax.broadcasted_iota(jnp.int32, (16, 16), 0) == across
    filled = jnp.sum(jnp.where(diagonal, counts[...], 0), axis=1, keepdims=True)
    alive = lax.broadcasted_iota(jnp.int32, (16, CAP), 1) < filled
    table[...] = jnp.zeros_like(table)
    table[0:16, 0:CAP] = jnp.where(alive, slots[...].astype(F32), -1.0)
    table[16:32, 0:CAP] = jnp.where(alive, probs[...], 0.0)
    names = pl.ds(0, 16)
    tz = {k: push(table.at[names], tab_z.at[back(k), names], at_z(k)) for k in (1, 3, 2)}
    ty = {k: push(table, tab_y.at[back(k)], at_y(k)) for k in (1, 3, 2)}
    drifts = [push(drift_ref.at[quarter(k), :], d_recv.at[back(k)], at_x(k)) for k in (2, 1, 3)]

    lane = lax.broadcasted_iota(jnp.int32, (CAP, 32), 1)
    token_of = lax.broadcasted_iota(jnp.int32, (CAP, TOK), 1).astype(F32)

    def column(tab, at):
        return jnp.sum(jnp.where(lane == at, tab, 0.0), axis=1, keepdims=True)

    def picked(tab, rows, expert, weighted):
        chosen = jnp.where(column(tab, expert) == token_of, 1.0, 0.0).astype(BF16)
        out = jnp.dot(chosen, rows, preferred_element_type=F32)
        if weighted:
            out = out * column(tab, expert + 16)
        return out.astype(BF16)

    chunk = {}
    relays = {}

    def scatter_x(kz):
        tab, rows = (tab_z[kz] if kz else table[...]).T[:CAP], tok_z[kz]
        for ky in (2, 1, 3, 0):
            expert = z * N + lax.rem(y + ky, N)
            got = picked(tab, rows, expert, False)
            if ky == 0:
                xs[kz, 0, :, :HALF] = got
                continue
            send_x[ky - 1, kz] = got
            src = send_x.at[ky - 1, kz]
            if ky == 2:
                relays["x", kz] = push(src, relay_x.at[kz], at_y(WAY[kz]))
            else:
                chunk["x", kz, back(ky)] = push(src, xs.at[kz, PLACE[back(ky)], :, mine], at_y(ky))

    def scatter_g(ky):
        tab, rows = (tab_y[ky] if ky else table[...]).T[:CAP], tg_y[ky]
        for kz in (2, 1, 3, 0):
            expert = lax.rem(z + kz, N) * N + y
            got = picked(tab, rows, expert, True)
            if kz == 0:
                gs[ky, 0, :, :HALF] = got
                continue
            send_g[kz - 1, ky] = got
            src = send_g.at[kz - 1, ky]
            if kz == 2:
                relays["g", ky] = push(src, relay_g.at[ky], at_z(WAY[ky]))
            else:
                chunk["g", ky, back(kz)] = push(src, gs.at[ky, PLACE[back(kz)], :, mine], at_z(kz))

    shared = {}

    def finish():
        for copy in started:
            copy.wait_recv()
            copy.wait_send()
        for copy in fetched:
            copy.wait()

    def share(name, group, members):
        for member in members:
            if member:
                chunk[name, group, member].wait_recv()
        buf = xs if name == "x" else gs
        places = pl.ds(PLACE[members[0]], len(members))
        shared.setdefault((name, group), []).append(
            push(buf.at[group, places, :, mine], buf.at[group, places, :, theirs], partner)
        )

    def relay(name, group):
        held, buf, at = (relay_x, xs, at_y) if name == "x" else (relay_g, gs, at_z)
        relays[name, group].wait_recv()
        chunk[name, group, 2] = push(
            held.at[group], buf.at[group, PLACE[2], :, mine], at(WAY[group])
        )

    def gate_group(kz):
        for copy in shared["x", kz]:
            copy.wait_recv()

        @pl.loop(0, HID // COLS)
        def _(n):
            cols = pl.ds(pl.multiple_of(n * COLS, COLS), COLS)
            v = jnp.dot(xs[kz].reshape(GROUP, FEAT), wg[:, cols], preferred_element_type=F32)
            gate[pl.ds(kz * GROUP, GROUP), cols] = v / (1.0 + jnp.exp(-v))

        @pl.loop(0, FEAT // TILE)
        def _(n):
            cols = pl.ds(pl.multiple_of(n * TILE, TILE), TILE)
            xt[cols, kz * GROUP : (kz + 1) * GROUP] = xs[kz, :, :, cols].reshape(GROUP, TILE).T

    nt = (((1,), (1,)), ((), ()))

    def back_group(ky):
        for copy in shared["g", ky]:
            copy.wait_recv()

        @pl.loop(0, HID // COLS)
        def _(n):
            cols = pl.ds(pl.multiple_of(n * COLS, COLS), COLS)
            v = lax.dot_general(
                gs[ky].reshape(GROUP, FEAT), wd[cols, :], nt, preferred_element_type=F32
            )
            backg[pl.ds(ky * GROUP, GROUP), cols] = v

    def hidden(kz, ky):
        rows = pl.ds(kz * GROUP + PLACE[ky] * CAP, CAP)
        others = pl.ds(ky * GROUP + PLACE[kz] * CAP, CAP)
        hid[rows, :] = (backg[others, :] * gate[rows, :]).astype(BF16)

    own_tok.wait()
    scatter_x(0)
    own_tg.wait()
    scatter_g(0)
    tok_up.wait_recv()
    tok_relay_up = push(tok_z.at[3, pl.ds(0, TOK // 2)], tok_z.at[2, pl.ds(0, TOK // 2)], at_z(1))
    tg_up.wait_recv()
    tg_relay_up = push(tg_y.at[3, pl.ds(0, TOK // 2)], tg_y.at[2, pl.ds(0, TOK // 2)], at_y(1))
    tok_down.wait_recv()
    tok_relay_down = push(
        tok_z.at[1, pl.ds(TOK // 2, TOK // 2)], tok_z.at[2, pl.ds(TOK // 2, TOK // 2)], at_z(3)
    )
    tg_down.wait_recv()
    tg_relay_down = push(
        tg_y.at[1, pl.ds(TOK // 2, TOK // 2)], tg_y.at[2, pl.ds(TOK // 2, TOK // 2)], at_y(3)
    )
    for k in (3, 1):
        tz[back(k)].wait_recv()
        scatter_x(k)
        ty[back(k)].wait_recv()
        scatter_g(k)
    relay("x", 0)
    relay("g", 0)
    share("x", 0, (0, 1, 3))
    share("g", 0, (0, 1, 3))
    tok_relay_up.wait_recv()
    tok_relay_down.wait_recv()
    tz[2].wait_recv()
    scatter_x(2)
    tg_relay_up.wait_recv()
    tg_relay_down.wait_recv()
    ty[2].wait_recv()
    scatter_g(2)
    relay("x", 3)
    relay("g", 3)
    share("x", 3, (0, 1, 3))
    share("g", 3, (0, 1, 3))
    relay("x", 1)
    relay("g", 1)
    share("x", 0, (2,))
    share("g", 0, (2,))
    share("x", 1, (0, 1, 3))
    share("g", 1, (0, 1, 3))
    for load in loads:
        load.wait()
    gate_group(0)
    back_group(0)
    hidden(0, 0)
    share("x", 3, (2,))
    share("g", 3, (2,))
    relay("x", 2)
    relay("g", 2)
    gate_group(3)
    back_group(3)
    share("x", 1, (2,))
    share("g", 1, (2,))
    share("x", 2, (0, 1, 3))
    share("g", 2, (0, 1, 3))
    share("x", 2, (2,))
    share("g", 2, (2,))
    gate_group(1)
    back_group(1)
    for kz in (0, 1, 3):
        for ky in (0, 1, 3):
            if kz or ky:
                hidden(kz, ky)
    gate_group(2)
    back_group(2)
    for k in (0, 1, 3):
        hidden(2, k)
        hidden(k, 2)
    hidden(2, 2)

    g_own, g_mine = gate.at[pl.ds(0, QUART)], gate.at[pl.ds(QUART, QUART)]
    g_far, g_near = wg.at[pl.ds(0, QUART)], wg.at[pl.ds(QUART, QUART)]
    g_join = wg.at[pl.ds(2 * QUART, QUART)]
    part[...] = jnp.zeros_like(part)

    def folded(v):
        s = jnp.sum(v.reshape(v.shape[0] // 8, 8, v.shape[1]), axis=0)
        return sum(s[:, i * 128 : (i + 1) * 128] for i in range(v.shape[1] // 128))

    def gradient(k, store, then=None):
        d = lax.rem(x + k, N)
        at = lax.rem(d // 2 + t, 2) * HALF + lax.rem(d, 2) * QUART
        rows = pl.ds(pl.multiple_of(at, QUART), QUART)

        def columns(cols):
            v = jnp.dot(xt[rows, :], hid[:, cols], preferred_element_type=F32)
            part[0] += folded(v * v)
            store(cols, v)

        if then is None:

            @pl.loop(0, HID // TILE)
            def _(n):
                columns(pl.ds(pl.multiple_of(n * TILE, TILE), TILE))

        else:
            for n in range(HID // TILE):
                columns(pl.ds(n * TILE, TILE))
                then(pl.ds(n * TILE, TILE))

    top, low = pl.ds(0, QUART // 2), pl.ds(QUART // 2, QUART // 2)

    def far(cols, v):
        g_far[:, cols] = v.astype(BF16)

    def up_side(cols, v):
        g_mine[top, cols] = v[: QUART // 2]
        g_near[top, cols] = v[QUART // 2 :].astype(BF16)

    def down_side(cols, v):
        g_near[low, cols] = v[: QUART // 2].astype(BF16)
        g_mine[low, cols] = v[QUART // 2 :]

    def keeping(cols, v):
        g_own[:, cols] = v

    far_copies = []

    def send_far(cols):
        far_copies.append(push(g_far.at[top, cols], g_relay.at[0, :, cols], at_x(1)))
        far_copies.append(push(g_far.at[low, cols], g_relay.at[1, :, cols], at_x(3)))

    gradient(2, far, send_far)
    gradient(1, up_side)
    first, second = pl.ds(0, QUART // 4), pl.ds(QUART // 4, QUART // 4)
    near = [push(g_near.at[pl.ds(0, QUART // 4)], g_direct.at[1, first], at_x(1))]
    gradient(3, down_side)
    near.append(push(g_near.at[pl.ds(QUART // 2, QUART // 4)], g_direct.at[0, first], at_x(3)))
    gradient(0, keeping)

    slot = [0]

    def gathered(value, pushes, then=lambda: None):
        first = slot[0]
        slot[0] += 1 + len(pushes)
        tiles[first] = value
        copies = []
        for i, (device, place) in enumerate(pushes):
            copies.append(push(tiles.at[first], tiles.at[first + place], device))
        then()
        for copy in copies:
            copy.wait_recv()
        return [tiles[first + i] for i in range(1 + len(pushes))]

    def ring(at):
        return [(at(k), back(k)) for k in (1, 2, 3)]

    def summed(v):
        return (v[0] + v[2]) + (v[1] + v[3])

    def group_sum(value):
        a = gathered(value, [(partner, 1)])
        b = summed(gathered(a[0] + a[1], ring(at_z)))
        return summed(gathered(b, ring(at_y)))

    def meanwhile():
        near.append(push(g_near.at[pl.ds(QUART // 4, QUART // 4)], g_direct.at[1, second], at_x(1)))
        near.append(push(g_near.at[pl.ds(3 * QUART // 4, QUART // 4)], g_direct.at[0, second], at_x(3)))

    square = group_sum(part[0])
    squares = gathered(square, ring(at_x), meanwhile)
    scales = []
    for v in squares:
        total = jnp.sum(jnp.sum(v, axis=1, keepdims=True), axis=0, keepdims=True)
        scales.append(jnp.minimum(1.0, math.sqrt(ENTRIES) / jnp.sqrt(total + 1e-06)))

    piece = QUART // 2 // PIECES
    joined = []
    for copy in far_copies:
        copy.wait_recv()
    for p in range(PIECES):
        rows = pl.ds(p * piece, piece)
        for side, way in ((0, 1), (1, 3)):
            from_there = scales[back(way)] * g_relay[side, rows, :].astype(F32)
            both = pl.ds(side * (QUART // 2) + p * piece, piece)
            g_join[both, :] = (from_there + scales[0] * g_mine[both, :]).astype(BF16)
            joined.append(push(g_join.at[both], g_recv.at[side, rows], at_x(way)))

    own_drift.wait()
    for copy in drifts:
        copy.wait_recv()
    for copy in near:
        copy.wait_recv()

    ups, downs = {}, {}
    for p in range(PIECES):
        for side in range(2):
            joined[2 * p + side].wait_recv()
            direct = scales[1] if side == 0 else scales[3]

            @pl.loop(0, piece // 64)
            def _(n):
                at = pl.multiple_of(p * piece + n * 64, 64)
                near = pl.ds(at, 64)
                rows = pl.ds(pl.multiple_of(side * (QUART // 2) + at, 64), 64)
                v = scales[0] * g_own[rows, :]
                v += direct * g_direct[side, near, :].astype(F32)
                v += g_recv[side, near, :].astype(F32)
                for k in range(N):
                    v += d_recv[k, rows, :].astype(F32)
                v = v * (1.0 / N)
                part[1] += folded(v * v)
                avg_all[0, rows, :] = v.astype(avg_all.dtype)

        at = {side: pl.ds(side * (QUART // 2) + p * piece, piece) for side in range(2)}
        for side in (0, 1):
            ups[p, side] = push(avg_all.at[0, at[side]], avg_all.at[3, at[side]], at_x(1))
        for side in (1, 0):
            downs[p, side] = push(avg_all.at[0, at[side]], avg_all.at[1, at[side]], at_x(3))

    fetch(avg_all.at[0], avg_ref.at[quarter(0), :])
    passed = []

    def pass_on(p):
        rows = pl.ds(p * piece, piece)
        ups[p, 0].wait_recv()
        passed.append(push(avg_all.at[3, rows], avg_all.at[2, rows], at_x(1)))
        rows = pl.ds(QUART // 2 + p * piece, piece)
        downs[p, 1].wait_recv()
        passed.append(push(avg_all.at[1, rows], avg_all.at[2, rows], at_x(3)))

    pass_on(0)
    b = group_sum(part[1])
    total = summed(gathered(b, ring(at_x)))
    total = jnp.sum(jnp.sum(total, axis=1, keepdims=True), axis=0, keepdims=True)
    scale = jnp.minimum(1.0, 0.25 * math.sqrt(ENTRIES) / jnp.sqrt(total + 1e-06))
    scale_ref[...] = jnp.broadcast_to(scale, scale_ref.shape)
    for p in range(1, PIECES):
        pass_on(p)
    for p in range(PIECES):
        ups[p, 1].wait_recv()
        downs[p, 0].wait_recv()
    fetch(avg_all.at[3], avg_ref.at[quarter(3), :])
    fetch(avg_all.at[1], avg_ref.at[quarter(1), :])
    for i, copy in enumerate(passed):
        copy.wait_recv()
        at = i % 2 * (QUART // 2) + i // 2 * piece
        there = pl.ds(pl.multiple_of(lax.rem(x + 2, N) * QUART + at, piece), piece)
        fetch(avg_all.at[2, pl.ds(at, piece)], avg_ref.at[there, :])
    finish()


def averaged(tokens, token_grads, slots, counts, probs, gate_weight, down_weight, drift):
    vm = pltpu.VMEM
    dma = pltpu.SemaphoreType.DMA
    return pl.pallas_call(
        kernel,
        out_shape=(
            jax.ShapeDtypeStruct((FEAT, HID), AVG),
            jax.ShapeDtypeStruct((8, 128), F32),
        ),
        in_specs=[pl.BlockSpec(memory_space=pl.ANY)] * 8,
        out_specs=(pl.BlockSpec(memory_space=pl.ANY), pl.BlockSpec(memory_space=pltpu.VMEM)),
        scratch_shapes=[
            vm((N, TOK, HALF), BF16),
            vm((N, TOK, HALF), BF16),
            vm((N, 32, 128), F32),
            vm((N, 32, 128), F32),
            vm((3, N, CAP, HALF), BF16),
            vm((3, N, CAP, HALF), BF16),
            vm((N, CAP, HALF), BF16),
            vm((N, CAP, HALF), BF16),
            vm((N, N, CAP, FEAT), BF16),
            vm((N, N, CAP, FEAT), BF16),
            vm((FEAT, HID), BF16),
            vm((HID, FEAT), BF16),
            vm((ROWS, HID), F32),
            vm((ROWS, HID), F32),
            vm((FEAT, ROWS), BF16),
            vm((ROWS, HID), BF16),
            vm((2, QUART // 2, HID), BF16),
            vm((2, QUART // 2, HID), BF16),
            vm((2, QUART // 2, HID), BF16),
            vm((N, QUART, HID), BF16),
            vm((N, QUART, HID), AVG),
            vm((2, 8, 128), F32),
            vm((32, 8, 128), F32),
            vm((16, CAP), jnp.int32),
            vm((1, 16), jnp.int32),
            vm((16, CAP), F32),
            vm((32, 128), F32),
            dma((SENDS,)),
            dma((COPIES,)),
            dma((17,)),
        ],
        compiler_params=pltpu.CompilerParams(
            collective_id=0, has_side_effects=True, vmem_limit_bytes=VMEM_AVERAGED
        ),
        name="averaged",
    )(tokens, token_grads, slots, counts, probs, gate_weight, down_weight, drift)


def last(scale_ref, avg_ref, old_ref, new_ref, step_ref, avg, new, step, sems):
    copies, reads = [], []
    for i in range(FEAT // LAST):
        rows = pl.ds(i * LAST, LAST)
        reads.append(pltpu.make_async_copy(avg_ref.at[rows], avg.at[rows], sems.at[2, i]))
        reads[-1].start()
    for i in range(FEAT // LAST):
        rows = pl.ds(i * LAST, LAST)
        reads[i].wait()
        clipped = scale_ref[0, 0] * avg[rows, :].astype(F32)
        moment = 0.9 * old_ref[rows, :] + clipped
        new[rows, :] = moment
        step[rows, :] = (0.7 * (clipped + 0.9 * moment)).astype(BF16)
        for j, (src, dst) in enumerate(((new, new_ref), (step, step_ref))):
            copies.append(pltpu.make_async_copy(src.at[rows], dst.at[rows], sems.at[j, i]))
            copies[-1].start()
    for copy in copies:
        copy.wait()


def updated(scale, average, momentum):
    place = pl.BlockSpec(memory_space=pltpu.VMEM)
    out = pl.BlockSpec(memory_space=pl.ANY)
    return pl.pallas_call(
        last,
        out_shape=(
            jax.ShapeDtypeStruct((FEAT, HID), F32),
            jax.ShapeDtypeStruct((FEAT, HID), BF16),
        ),
        in_specs=[pl.BlockSpec(memory_space=pltpu.SMEM), out, place],
        out_specs=(out, out),
        scratch_shapes=[
            pltpu.VMEM((FEAT, HID), AVG),
            pltpu.VMEM((FEAT, HID), F32),
            pltpu.VMEM((FEAT, HID), BF16),
            pltpu.SemaphoreType.DMA((3, FEAT // LAST)),
        ],
        compiler_params=pltpu.CompilerParams(vmem_limit_bytes=VMEM_UPDATED),
        name="updated",
    )(scale, average, momentum)


def body(
    tokens,
    token_grads,
    slot_token,
    slot_count,
    slot_prob,
    gate_weight,
    down_weight,
    drift,
    momentum,
):
    average, scale = averaged(
        tokens[0], token_grads[0], slot_token[0, 0], slot_count[0], slot_prob[0, 0],
        gate_weight[0, 0], down_weight[0, 0], drift[0, 0],
    )
    new_momentum, outer_step = updated(scale, average, momentum[0])
    return (new_momentum[None], outer_step[None])


def solution(mesh):
    return jax.shard_map(
        body,
        mesh=mesh,
        in_specs=(
            P("island", "expert", "tensor"),
            P("island", "expert", "tensor"),
            P("island", "expert", None, None),
            P("island", "expert", None),
            P("island", "expert", None, None),
            P("island", "expert", None, "tensor"),
            P("island", "expert", "tensor", None),
            P("island", "expert", None, "tensor"),
            P("expert", None, "tensor"),
        ),
        out_specs=(P("expert", None, "tensor"), P("expert", None, "tensor")),
        check_vma=False,
    )
```

```python
import functools
import math

import jax
import jax.numpy as jnp
from jax import lax
from jax.experimental import pallas as pl
from jax.experimental.pallas import tpu as pltpu
from jax.sharding import PartitionSpec as P

MESH = pl.DeviceIdType.MESH
BF16 = jnp.bfloat16
F32 = jnp.float32
AVG = jnp.bfloat16
N = 4
CAP = 96
GROUP = N * CAP
ROWS = N * GROUP
TOK = 256
HALF = 1024
FEAT = 2 * HALF
QUART = FEAT // N
HID = 768
TILE = 256
COLS = 256
PIECES = 2
VMEM_AVERAGED = 55 << 20
VMEM_UPDATED = 57 << 20
WAY = (1, 3, 1, 3)
PLACE = (0, 1, 3, 2)
SENDS = 88
COPIES = 111
LAST = 256
ENTRIES = 16 * 2048 * 1536


def back(k):
    return (N - k) % N


class Sent:
    def __init__(self, copy):
        self.copy, self.arrived, self.sent = copy, False, False

    def wait(self):
        if not self.arrived:
            self.copy.wait()
        self.arrived = True

    def wait_recv(self):
        if not self.arrived:
            self.copy.wait_recv()
        self.arrived = True

    def wait_send(self):
        if not self.sent:
            self.copy.wait_send()
        self.sent = True


def kernel(
    tok_ref, tg_ref, slot_ref, count_ref, prob_ref, wg_ref, wd_ref, drift_ref,
    avg_ref, scale_ref,
    tok_z, tg_y, tab_z, tab_y, send_x, send_g, relay_x, relay_g, xs, gs, wg, wd,
    gate, backg, xt, hid, g_relay, g_direct, g_recv, d_recv, avg_all,
    part, tiles, slots, counts, probs, table, send_sem, recv_sem, local_sem,
):
    x = lax.axis_index("island")
    ex = lax.axis_index("expert")
    t = lax.axis_index("tensor")
    z, y = ex // N, lax.rem(ex, N)

    def at_x(k):
        return {"island": lax.rem(x + k, N)}

    def at_z(k):
        return {"expert": lax.rem(z + k, N) * N + y}

    def at_y(k):
        return {"expert": z * N + lax.rem(y + k, N)}

    partner = {"tensor": 1 - t}
    started, fetched = [], []

    def push(src, dst, device):
        i = len(started)
        if i >= SENDS:
            started[i - SENDS].wait_send()
        copy = pltpu.make_async_remote_copy(
            src_ref=src, dst_ref=dst, send_sem=send_sem.at[i % SENDS], recv_sem=recv_sem.at[i],
            device_id=device, device_id_type=MESH,
        )
        copy.start()
        started.append(Sent(copy))
        return started[-1]

    def fetch(src, dst):
        copy = pltpu.make_async_copy(src, dst, local_sem.at[len(fetched)])
        copy.start()
        fetched.append(Sent(copy))
        return fetched[-1]

    own_slots = [fetch(slot_ref, slots), fetch(count_ref, counts), fetch(prob_ref, probs)]
    own_tok = fetch(tok_ref, tok_z.at[0])
    own_tg = fetch(tg_ref, tg_y.at[0])
    mine, theirs = pl.ds(0, HALF), pl.ds(HALF, HALF)
    own_half = pl.ds(pl.multiple_of(t * HALF, HALF), HALF)
    other_half = pl.ds(pl.multiple_of((1 - t) * HALF, HALF), HALF)
    loads = [
        fetch(wg_ref.at[own_half, :], wg.at[mine, :]),
        fetch(wg_ref.at[other_half, :], wg.at[theirs, :]),
        fetch(wd_ref.at[:, own_half], wd.at[:, mine]),
        fetch(wd_ref.at[:, other_half], wd.at[:, theirs]),
    ]

    def quarter(k):
        return pl.ds(pl.multiple_of(lax.rem(x + k, N) * QUART, QUART), QUART)

    own_drift = fetch(drift_ref.at[quarter(0), :], d_recv.at[0])

    barrier = pltpu.get_barrier_semaphore()
    peers = [at(k) for at in (at_x, at_y, at_z) for k in (1, 2, 3)] + [partner]
    for peer in peers:
        pl.semaphore_signal(barrier, inc=1, device_id=peer, device_id_type=MESH)
    pl.semaphore_wait(barrier, len(peers))

    tok_up = push(tok_ref, tok_z.at[3], at_z(1))
    tok_down = push(tok_ref, tok_z.at[1], at_z(3))
    tg_up = push(tg_ref, tg_y.at[3], at_y(1))
    tg_down = push(tg_ref, tg_y.at[1], at_y(3))
    for copy in own_slots:
        copy.wait()
    across = lax.broadcasted_iota(jnp.int32, (16, 16), 1)
    diagonal = lax.broadcasted_iota(jnp.int32, (16, 16), 0) == across
    filled = jnp.sum(jnp.where(diagonal, counts[...], 0), axis=1, keepdims=True)
    alive = lax.broadcasted_iota(jnp.int32, (16, CAP), 1) < filled
    table[...] = jnp.zeros_like(table)
    table[0:16, 0:CAP] = jnp.where(alive, slots[...].astype(F32), -1.0)
    table[16:32, 0:CAP] = jnp.where(alive, probs[...], 0.0)
    names = pl.ds(0, 16)
    tz = {k: push(table.at[names], tab_z.at[back(k), names], at_z(k)) for k in (1, 3, 2)}
    ty = {k: push(table, tab_y.at[back(k)], at_y(k)) for k in (1, 3, 2)}
    drifts = [push(drift_ref.at[quarter(k), :], d_recv.at[back(k)], at_x(k)) for k in (2, 1, 3)]

    lane = lax.broadcasted_iota(jnp.int32, (CAP, 32), 1)
    token_of = lax.broadcasted_iota(jnp.int32, (CAP, TOK), 1).astype(F32)

    def column(tab, at):
        return jnp.sum(jnp.where(lane == at, tab, 0.0), axis=1, keepdims=True)

    def picked(tab, rows, expert, weighted):
        chosen = jnp.where(column(tab, expert) == token_of, 1.0, 0.0).astype(BF16)
        out = jnp.dot(chosen, rows, preferred_element_type=F32)
        if weighted:
            out = out * column(tab, expert + 16)
        return out.astype(BF16)

    chunk = {}
    relays = {}

    def scatter_x(kz):
        tab, rows = (tab_z[kz] if kz else table[...]).T[:CAP], tok_z[kz]
        for ky in (2, 1, 3, 0):
            expert = z * N + lax.rem(y + ky, N)
            got = picked(tab, rows, expert, False)
            if ky == 0:
                xs[kz, 0, :, :HALF] = got
                continue
            send_x[ky - 1, kz] = got
            src = send_x.at[ky - 1, kz]
            if ky == 2:
                relays["x", kz] = push(src, relay_x.at[kz], at_y(WAY[kz]))
            else:
                chunk["x", kz, back(ky)] = push(src, xs.at[kz, PLACE[back(ky)], :, mine], at_y(ky))

    def scatter_g(ky):
        tab, rows = (tab_y[ky] if ky else table[...]).T[:CAP], tg_y[ky]
        for kz in (2, 1, 3, 0):
            expert = lax.rem(z + kz, N) * N + y
            got = picked(tab, rows, expert, True)
            if kz == 0:
                gs[ky, 0, :, :HALF] = got
                continue
            send_g[kz - 1, ky] = got
            src = send_g.at[kz - 1, ky]
            if kz == 2:
                relays["g", ky] = push(src, relay_g.at[ky], at_z(WAY[ky]))
            else:
                chunk["g", ky, back(kz)] = push(src, gs.at[ky, PLACE[back(kz)], :, mine], at_z(kz))

    shared = {}

    def finish():
        for copy in started:
            copy.wait_recv()
            copy.wait_send()
        for copy in fetched:
            copy.wait()

    def share(name, group, members):
        for member in members:
            if member:
                chunk[name, group, member].wait_recv()
        buf = xs if name == "x" else gs
        places = pl.ds(PLACE[members[0]], len(members))
        shared.setdefault((name, group), []).append(
            push(buf.at[group, places, :, mine], buf.at[group, places, :, theirs], partner)
        )

    def relay(name, group):
        held, buf, at = (relay_x, xs, at_y) if name == "x" else (relay_g, gs, at_z)
        relays[name, group].wait_recv()
        chunk[name, group, 2] = push(
            held.at[group], buf.at[group, PLACE[2], :, mine], at(WAY[group])
        )

    def gate_group(kz):
        for copy in shared["x", kz]:
            copy.wait_recv()

        @pl.loop(0, HID // COLS)
        def _(n):
            cols = pl.ds(pl.multiple_of(n * COLS, COLS), COLS)
            v = jnp.dot(xs[kz].reshape(GROUP, FEAT), wg[:, cols], preferred_element_type=F32)
            gate[pl.ds(kz * GROUP, GROUP), cols] = v / (1.0 + jnp.exp(-v))

        @pl.loop(0, FEAT // TILE)
        def _(n):
            cols = pl.ds(pl.multiple_of(n * TILE, TILE), TILE)
            xt[cols, kz * GROUP : (kz + 1) * GROUP] = xs[kz, :, :, cols].reshape(GROUP, TILE).T

    nt = (((1,), (1,)), ((), ()))

    def back_group(ky):
        for copy in shared["g", ky]:
            copy.wait_recv()

        @pl.loop(0, HID // COLS)
        def _(n):
            cols = pl.ds(pl.multiple_of(n * COLS, COLS), COLS)
            v = lax.dot_general(
                gs[ky].reshape(GROUP, FEAT), wd[cols, :], nt, preferred_element_type=F32
            )
            backg[pl.ds(ky * GROUP, GROUP), cols] = v

    def hidden(kz, ky):
        rows = pl.ds(kz * GROUP + PLACE[ky] * CAP, CAP)
        others = pl.ds(ky * GROUP + PLACE[kz] * CAP, CAP)
        hid[rows, :] = (backg[others, :] * gate[rows, :]).astype(BF16)

    own_tok.wait()
    scatter_x(0)
    own_tg.wait()
    scatter_g(0)
    tok_up.wait_recv()
    tok_relay_up = push(tok_z.at[3, pl.ds(0, TOK // 2)], tok_z.at[2, pl.ds(0, TOK // 2)], at_z(1))
    tg_up.wait_recv()
    tg_relay_up = push(tg_y.at[3, pl.ds(0, TOK // 2)], tg_y.at[2, pl.ds(0, TOK // 2)], at_y(1))
    tok_down.wait_recv()
    tok_relay_down = push(
        tok_z.at[1, pl.ds(TOK // 2, TOK // 2)], tok_z.at[2, pl.ds(TOK // 2, TOK // 2)], at_z(3)
    )
    tg_down.wait_recv()
    tg_relay_down = push(
        tg_y.at[1, pl.ds(TOK // 2, TOK // 2)], tg_y.at[2, pl.ds(TOK // 2, TOK // 2)], at_y(3)
    )
    for k in (3, 1):
        tz[back(k)].wait_recv()
        scatter_x(k)
        ty[back(k)].wait_recv()
        scatter_g(k)
    relay("x", 0)
    relay("g", 0)
    share("x", 0, (0, 1, 3))
    share("g", 0, (0, 1, 3))
    tok_relay_up.wait_recv()
    tok_relay_down.wait_recv()
    tz[2].wait_recv()
    scatter_x(2)
    tg_relay_up.wait_recv()
    tg_relay_down.wait_recv()
    ty[2].wait_recv()
    scatter_g(2)
    relay("x", 3)
    relay("g", 3)
    share("x", 3, (0, 1, 3))
    share("g", 3, (0, 1, 3))
    relay("x", 1)
    relay("g", 1)
    share("x", 0, (2,))
    share("g", 0, (2,))
    share("x", 1, (0, 1, 3))
    share("g", 1, (0, 1, 3))
    for load in loads:
        load.wait()
    gate_group(0)
    back_group(0)
    hidden(0, 0)
    share("x", 3, (2,))
    share("g", 3, (2,))
    relay("x", 2)
    relay("g", 2)
    gate_group(3)
    back_group(3)
    share("x", 1, (2,))
    share("g", 1, (2,))
    share("x", 2, (0, 1, 3))
    share("g", 2, (0, 1, 3))
    share("x", 2, (2,))
    share("g", 2, (2,))
    gate_group(1)
    back_group(1)
    for kz in (0, 1, 3):
        for ky in (0, 1, 3):
            if kz or ky:
                hidden(kz, ky)
    gate_group(2)
    back_group(2)
    for k in (0, 1, 3):
        hidden(2, k)
        hidden(k, 2)
    hidden(2, 2)

    g_own, g_mine = gate.at[pl.ds(0, QUART)], gate.at[pl.ds(QUART, QUART)]
    g_far, g_near = wg.at[pl.ds(0, QUART)], wg.at[pl.ds(QUART, QUART)]
    g_join = wg.at[pl.ds(2 * QUART, QUART)]
    part[...] = jnp.zeros_like(part)

    def folded(v):
        s = jnp.sum(v.reshape(v.shape[0] // 8, 8, v.shape[1]), axis=0)
        return sum(s[:, i * 128 : (i + 1) * 128] for i in range(v.shape[1] // 128))

    def gradient(k, store, then=None):
        d = lax.rem(x + k, N)
        at = lax.rem(d // 2 + t, 2) * HALF + lax.rem(d, 2) * QUART
        rows = pl.ds(pl.multiple_of(at, QUART), QUART)

        def columns(cols):
            v = jnp.dot(xt[rows, :], hid[:, cols], preferred_element_type=F32)
            part[0] += folded(v * v)
            store(cols, v)

        if then is None:

            @pl.loop(0, HID // TILE)
            def _(n):
                columns(pl.ds(pl.multiple_of(n * TILE, TILE), TILE))

        else:
            for n in range(HID // TILE):
                columns(pl.ds(n * TILE, TILE))
                then(pl.ds(n * TILE, TILE))

    top, low = pl.ds(0, QUART // 2), pl.ds(QUART // 2, QUART // 2)

    def far(cols, v):
        g_far[:, cols] = v.astype(BF16)

    def up_side(cols, v):
        g_mine[top, cols] = v[: QUART // 2]
        g_near[top, cols] = v[QUART // 2 :].astype(BF16)

    def down_side(cols, v):
        g_near[low, cols] = v[: QUART // 2].astype(BF16)
        g_mine[low, cols] = v[QUART // 2 :]

    def keeping(cols, v):
        g_own[:, cols] = v

    far_copies = []

    def send_far(cols):
        far_copies.append(push(g_far.at[top, cols], g_relay.at[0, :, cols], at_x(1)))
        far_copies.append(push(g_far.at[low, cols], g_relay.at[1, :, cols], at_x(3)))

    gradient(2, far, send_far)
    gradient(1, up_side)
    first, second = pl.ds(0, QUART // 4), pl.ds(QUART // 4, QUART // 4)
    near = [push(g_near.at[pl.ds(0, QUART // 4)], g_direct.at[1, first], at_x(1))]
    gradient(3, down_side)
    near.append(push(g_near.at[pl.ds(QUART // 2, QUART // 4)], g_direct.at[0, first], at_x(3)))
    gradient(0, keeping)

    slot = [0]

    def gathered(value, pushes, then=lambda: None):
        first = slot[0]
        slot[0] += 1 + len(pushes)
        tiles[first] = value
        copies = []
        for i, (device, place) in enumerate(pushes):
            copies.append(push(tiles.at[first], tiles.at[first + place], device))
        then()
        for copy in copies:
            copy.wait_recv()
        return [tiles[first + i] for i in range(1 + len(pushes))]

    def ring(at):
        return [(at(k), back(k)) for k in (1, 2, 3)]

    def summed(v):
        return (v[0] + v[2]) + (v[1] + v[3])

    def group_sum(value):
        a = gathered(value, [(partner, 1)])
        b = summed(gathered(a[0] + a[1], ring(at_z)))
        return summed(gathered(b, ring(at_y)))

    def meanwhile():
        near.append(push(g_near.at[pl.ds(QUART // 4, QUART // 4)], g_direct.at[1, second], at_x(1)))
        near.append(push(g_near.at[pl.ds(3 * QUART // 4, QUART // 4)], g_direct.at[0, second], at_x(3)))

    square = group_sum(part[0])
    squares = gathered(square, ring(at_x), meanwhile)
    scales = []
    for v in squares:
        total = jnp.sum(jnp.sum(v, axis=1, keepdims=True), axis=0, keepdims=True)
        scales.append(jnp.minimum(1.0, math.sqrt(ENTRIES) / jnp.sqrt(total + 1e-06)))

    piece = QUART // 2 // PIECES
    joined = []
    for copy in far_copies:
        copy.wait_recv()
    for p in range(PIECES):
        rows = pl.ds(p * piece, piece)
        for side, way in ((0, 1), (1, 3)):
            from_there = scales[back(way)] * g_relay[side, rows, :].astype(F32)
            both = pl.ds(side * (QUART // 2) + p * piece, piece)
            g_join[both, :] = (from_there + scales[0] * g_mine[both, :]).astype(BF16)
            joined.append(push(g_join.at[both], g_recv.at[side, rows], at_x(way)))

    own_drift.wait()
    for copy in drifts:
        copy.wait_recv()
    for copy in near:
        copy.wait_recv()

    ups, downs = {}, {}
    for p in range(PIECES):
        for side in range(2):
            joined[2 * p + side].wait_recv()
            direct = scales[1] if side == 0 else scales[3]

            @pl.loop(0, piece // 64)
            def _(n):
                at = pl.multiple_of(p * piece + n * 64, 64)
                near = pl.ds(at, 64)
                rows = pl.ds(pl.multiple_of(side * (QUART // 2) + at, 64), 64)
                v = scales[0] * g_own[rows, :]
                v += direct * g_direct[side, near, :].astype(F32)
                v += g_recv[side, near, :].astype(F32)
                for k in range(N):
                    v += d_recv[k, rows, :].astype(F32)
                v = v * (1.0 / N)
                part[1] += folded(v * v)
                avg_all[0, rows, :] = v.astype(avg_all.dtype)

        at = {side: pl.ds(side * (QUART // 2) + p * piece, piece) for side in range(2)}
        for side in (0, 1):
            ups[p, side] = push(avg_all.at[0, at[side]], avg_all.at[3, at[side]], at_x(1))
        for side in (1, 0):
            downs[p, side] = push(avg_all.at[0, at[side]], avg_all.at[1, at[side]], at_x(3))

    fetch(avg_all.at[0], avg_ref.at[quarter(0), :])
    passed = []

    def pass_on(p):
        rows = pl.ds(p * piece, piece)
        ups[p, 0].wait_recv()
        passed.append(push(avg_all.at[3, rows], avg_all.at[2, rows], at_x(1)))
        rows = pl.ds(QUART // 2 + p * piece, piece)
        downs[p, 1].wait_recv()
        passed.append(push(avg_all.at[1, rows], avg_all.at[2, rows], at_x(3)))

    pass_on(0)
    b = group_sum(part[1])
    total = summed(gathered(b, ring(at_x)))
    total = jnp.sum(jnp.sum(total, axis=1, keepdims=True), axis=0, keepdims=True)
    scale = jnp.minimum(1.0, 0.25 * math.sqrt(ENTRIES) / jnp.sqrt(total + 1e-06))
    scale_ref[...] = jnp.broadcast_to(scale, scale_ref.shape)
    for p in range(1, PIECES):
        pass_on(p)
    for p in range(PIECES):
        ups[p, 1].wait_recv()
        downs[p, 0].wait_recv()
    fetch(avg_all.at[3], avg_ref.at[quarter(3), :])
    fetch(avg_all.at[1], avg_ref.at[quarter(1), :])
    for i, copy in enumerate(passed):
        copy.wait_recv()
        at = i % 2 * (QUART // 2) + i // 2 * piece
        there = pl.ds(pl.multiple_of(lax.rem(x + 2, N) * QUART + at, piece), piece)
        fetch(avg_all.at[2, pl.ds(at, piece)], avg_ref.at[there, :])
    finish()


def averaged(tokens, token_grads, slots, counts, probs, gate_weight, down_weight, drift):
    vm = pltpu.VMEM
    dma = pltpu.SemaphoreType.DMA
    return pl.pallas_call(
        kernel,
        out_shape=(
            jax.ShapeDtypeStruct((FEAT, HID), AVG),
            jax.ShapeDtypeStruct((8, 128), F32),
        ),
        in_specs=[pl.BlockSpec(memory_space=pl.ANY)] * 8,
        out_specs=(pl.BlockSpec(memory_space=pl.ANY), pl.BlockSpec(memory_space=pltpu.VMEM)),
        scratch_shapes=[
            vm((N, TOK, HALF), BF16),
            vm((N, TOK, HALF), BF16),
            vm((N, 32, 128), F32),
            vm((N, 32, 128), F32),
            vm((3, N, CAP, HALF), BF16),
            vm((3, N, CAP, HALF), BF16),
            vm((N, CAP, HALF), BF16),
            vm((N, CAP, HALF), BF16),
            vm((N, N, CAP, FEAT), BF16),
            vm((N, N, CAP, FEAT), BF16),
            vm((FEAT, HID), BF16),
            vm((HID, FEAT), BF16),
            vm((ROWS, HID), F32),
            vm((ROWS, HID), F32),
            vm((FEAT, ROWS), BF16),
            vm((ROWS, HID), BF16),
            vm((2, QUART // 2, HID), BF16),
            vm((2, QUART // 2, HID), BF16),
            vm((2, QUART // 2, HID), BF16),
            vm((N, QUART, HID), BF16),
            vm((N, QUART, HID), AVG),
            vm((2, 8, 128), F32),
            vm((32, 8, 128), F32),
            vm((16, CAP), jnp.int32),
            vm((1, 16), jnp.int32),
            vm((16, CAP), F32),
            vm((32, 128), F32),
            dma((SENDS,)),
            dma((COPIES,)),
            dma((17,)),
        ],
        compiler_params=pltpu.CompilerParams(
            collective_id=0, has_side_effects=True, vmem_limit_bytes=VMEM_AVERAGED
        ),
        name="averaged",
    )(tokens, token_grads, slots, counts, probs, gate_weight, down_weight, drift)


def last(scale_ref, avg_ref, old_ref, new_ref, step_ref, avg, new, step, sems):
    copies, reads = [], []
    for i in range(FEAT // LAST):
        rows = pl.ds(i * LAST, LAST)
        reads.append(pltpu.make_async_copy(avg_ref.at[rows], avg.at[rows], sems.at[2, i]))
        reads[-1].start()
    for i in range(FEAT // LAST):
        rows = pl.ds(i * LAST, LAST)
        reads[i].wait()
        clipped = scale_ref[0, 0] * avg[rows, :].astype(F32)
        moment = 0.9 * old_ref[rows, :] + clipped
        new[rows, :] = moment
        step[rows, :] = (0.7 * (clipped + 0.9 * moment)).astype(BF16)
        for j, (src, dst) in enumerate(((new, new_ref), (step, step_ref))):
            copies.append(pltpu.make_async_copy(src.at[rows], dst.at[rows], sems.at[j, i]))
            copies[-1].start()
    for copy in copies:
        copy.wait()


def updated(scale, average, momentum):
    place = pl.BlockSpec(memory_space=pltpu.VMEM)
    out = pl.BlockSpec(memory_space=pl.ANY)
    return pl.pallas_call(
        last,
        out_shape=(
            jax.ShapeDtypeStruct((FEAT, HID), F32),
            jax.ShapeDtypeStruct((FEAT, HID), BF16),
        ),
        in_specs=[pl.BlockSpec(memory_space=pltpu.SMEM), out, place],
        out_specs=(out, out),
        scratch_shapes=[
            pltpu.VMEM((FEAT, HID), AVG),
            pltpu.VMEM((FEAT, HID), F32),
            pltpu.VMEM((FEAT, HID), BF16),
            pltpu.SemaphoreType.DMA((3, FEAT // LAST)),
        ],
        compiler_params=pltpu.CompilerParams(vmem_limit_bytes=VMEM_UPDATED),
        name="updated",
    )(scale, average, momentum)


def body(
    tokens,
    token_grads,
    slot_token,
    slot_count,
    slot_prob,
    gate_weight,
    down_weight,
    drift,
    momentum,
):
    average, scale = averaged(
        tokens[0], token_grads[0], slot_token[0, 0], slot_count[0], slot_prob[0, 0],
        gate_weight[0, 0], down_weight[0, 0], drift[0, 0],
    )
    new_momentum, outer_step = updated(scale, average, momentum[0])
    return (new_momentum[None], outer_step[None])


def solution(mesh):
    return jax.shard_map(
        body,
        mesh=mesh,
        in_specs=(
            P("island", "expert", "tensor"),
            P("island", "expert", "tensor"),
            P("island", "expert", None, None),
            P("island", "expert", None),
            P("island", "expert", None, None),
            P("island", "expert", None, "tensor"),
            P("island", "expert", "tensor", None),
            P("island", "expert", None, "tensor"),
            P("expert", None, "tensor"),
        ),
        out_specs=(P("expert", None, "tensor"), P("expert", None, "tensor")),
        check_vma=False,
    )
```
